512 devices in a mesh: group: 8 (over z_lo), blk: 64 (over y, z_hi, x, core).
Axes of the slice: x: 4, y: 4, z: 16 (z_hi: 2, z_lo: 8; z = z_hi * 8 + z_lo), core: 2. Of those that a mesh axis runs over, the one named last changes fastest.
Arguments:
- traces: bfloat16 [2048, 3, 2, 1200], P(('group', 'blk')), may hold values from -180 to 180, as said below
- assign: int32 [2048], P(('group', 'blk')), may hold values from 0 to 3, as said below
- matching: int32 [64, 8], P('blk'), may hold values from 0 to 7, as said below
Outputs:
- between: bfloat16 [2048, 4, 3, 3, 401], P(('group', 'blk'))
- within: bfloat16 [2048, 4, 3, 3, 401], P(('group', 'blk'))
The draws below stay inside these ranges and needn't reach their ends.
Inputs may be any that keep to these rules, and one draw needn't show every extreme that they name: traces are finite records. `assign`: each aligned block of 4 entries, one device's stations, is a permutation of 0 to 3. `matching`: each row b is one round r_b, 0 to 7, of a round-robin plan with a bye round 0: group g is paired with g XOR r_b.
All inputs are finite; a program needn't handle non-finite values.
Results may differ from the reference program's by a relative error of at most 0.0082.
Values may be sent and summed in bfloat16 or wider, within the bound.
A program may use at most 64 MiB of HBM per device.

```python
import math
import jax
import jax.numpy as jnp
from jax import lax

STA_DEV = 4
WIN = 2
NSAMP = 1200
PLEN = 1536
NF = 768
HALF = 200
LAGS = 401
GROUPS = 8
BLOCKS = 64
STATIONS = 2048
N_BLK = 64


def draw_traces(key, part):
    noise_key = jax.random.fold_in(key, 11)
    scale_key = jax.random.fold_in(key, 13)
    noise_values = jnp.clip(jax.random.normal(noise_key, (STATIONS, 3, WIN, NSAMP), jnp.float32), -6.0, 6.0)
    log_scales = jax.random.uniform(scale_key, (STATIONS, 3, WIN, 1), jnp.float32, 0.0, math.log(10.0))
    return (noise_values * jnp.exp(log_scales)).astype(jnp.bfloat16)


def permute_block(block_key):
    return jax.random.permutation(block_key, STA_DEV)


def draw_assign(key, part):
    block_keys = jax.random.split(jax.random.fold_in(key, 23), STATIONS // STA_DEV)
    return jax.vmap(permute_block)(block_keys).reshape(-1).astype(jnp.int32)


def draw_matching(key, part):
    rounds = jax.random.randint(jax.random.fold_in(key, 37), (BLOCKS, 1), 0, GROUPS).astype(jnp.int32)
    players = jnp.arange(GROUPS, dtype=jnp.int32)[None, :]
    return jnp.bitwise_xor(players, rounds).astype(jnp.int32)


def setup_inputs(seed: int = 0) -> dict:
    splits = jax.random.split(jax.random.key(seed), 4)
    traces = draw_traces(jax.random.fold_in(splits[3], 71), 0)
    assign = draw_assign(jax.random.fold_in(splits[3], 71), 0)
    matching = draw_matching(jax.random.fold_in(splits[3], 71), 0)
    return {"traces": traces, "assign": assign, "matching": matching}


EPSILON = 1e-05

def forward_table():
    sample_ids = jnp.arange(NSAMP, dtype=jnp.int32)[:, None]
    bin_ids = jnp.arange(1, NF + 1, dtype=jnp.int32)[None, :]
    phases = (sample_ids * bin_ids % PLEN).astype(jnp.float32) * (2.0 * math.pi / PLEN)
    return jnp.concatenate([jnp.cos(phases), -jnp.sin(phases)], axis=1).astype(jnp.bfloat16)

def inverse_table():
    bin_ids = jnp.arange(1, NF + 1, dtype=jnp.int32)[:, None]
    lag_ids = jnp.arange(LAGS, dtype=jnp.int32)[None, :] - HALF
    phases = (bin_ids * lag_ids % PLEN).astype(jnp.float32) * (2.0 * math.pi / PLEN)
    return jnp.concatenate([jnp.cos(phases), -jnp.sin(phases)], axis=0).astype(jnp.bfloat16)

def correlate(local_spec, remote_spec, inverse):
    left = local_spec.astype(jnp.float32)
    right = remote_spec.astype(jnp.float32)
    left_re, left_im = (left[..., :NF], left[..., NF:])
    right_re, right_im = (right[..., :NF], right[..., NF:])

    def outer_sum(first_part, second_part):
        return jnp.einsum('acwk,bdwk->abcdk', first_part, second_part)
    real_part = outer_sum(left_re, right_re) + outer_sum(left_im, right_im)
    imag_part = outer_sum(left_re, right_im) - outer_sum(left_im, right_re)
    stacked = jnp.concatenate([real_part, imag_part], axis=-1).astype(jnp.bfloat16)
    lag_scale = 2.0 / (PLEN * math.sqrt(NSAMP * WIN))
    lag_values = jnp.dot(stacked.reshape(-1, 2 * NF), inverse, preferred_element_type=jnp.float32) * lag_scale
    return lag_values.astype(jnp.bfloat16).reshape(STA_DEV, STA_DEV, 3, 3, LAGS)

def reference(traces, assign, matching):
    device_total = STATIONS // STA_DEV
    row_ids = jnp.arange(STATIONS, dtype=jnp.int32)
    block_base = row_ids // STA_DEV * STA_DEV
    source_rows = jnp.zeros((STATIONS,), jnp.int32).at[block_base + assign].set(row_ids)
    ordered = traces[source_rows]
    values = ordered.astype(jnp.float32)
    energy = lax.optimization_barrier(jnp.mean(values * values, axis=-1, keepdims=True))
    normal = (values * lax.rsqrt(energy + EPSILON)).astype(jnp.bfloat16)
    forward = forward_table()
    inverse = inverse_table()
    spectra = jnp.dot(normal.reshape(-1, NSAMP), forward, preferred_element_type=jnp.float32)
    spectra = spectra.astype(jnp.bfloat16).reshape(device_total, STA_DEV, 3, WIN, PLEN)
    device_ids = jnp.arange(device_total, dtype=jnp.int32)
    group_ids = device_ids // N_BLK
    blk_ids = device_ids % N_BLK
    partner = matching[blk_ids, group_ids] * N_BLK + blk_ids
    neighbour = group_ids * N_BLK + (blk_ids - 1) % N_BLK

    def per_device(device):
        local_spec = spectra[device]
        return (correlate(local_spec, spectra[partner[device]], inverse), correlate(local_spec, spectra[neighbour[device]], inverse))
    between, within = lax.map(per_device, device_ids)
    return (between.reshape(STATIONS, STA_DEV, 3, 3, LAGS), within.reshape(STATIONS, STA_DEV, 3, 3, LAGS))
```

```python
import functools
import math

import jax
import jax.numpy as jnp
import ml_dtypes
import numpy as np
from jax import lax
from jax.experimental import pallas as pl
from jax.experimental.pallas import tpu as pltpu
from jax.sharding import PartitionSpec as P

WIN = 2
NSAMP = 1200
PLEN = 1536
NF = 768
HALF = 200
LAGS = 401
FAST = 256
EPSILON = 1e-05
SCALE = 2.0 / (PLEN * math.sqrt(NSAMP * WIN))
ROOT3 = math.sqrt(3) / 2
MESH = pl.DeviceIdType.MESH
bf16, f32 = jnp.bfloat16, jnp.float32

FIRSTS = ((1, 256), (2, 256), (3, 128), (6, 128))
BINS = np.concatenate([first + 6 * np.arange(count) for first, count in FIRSTS])


def tables():
    n = np.arange(FAST)
    phases = 2 * np.pi * (np.outer(n, n) % FAST) / FAST
    c, s = np.cos(phases), np.sin(phases)
    full = np.block([[c, -s], [s, c]])
    half = np.concatenate([full[:, :128], full[:, 256:384]], axis=1)
    twiddle = np.zeros((64, FAST), np.float32)
    for i, (first, _) in enumerate(FIRSTS):
        phases = 2 * np.pi * n * first / PLEN
        twiddle[16 * i : 16 * i + 8] = np.cos(phases)
        twiddle[16 * i + 8 : 16 * i + 16] = np.sin(phases)
    phases = 2 * np.pi * (np.outer(BINS, np.arange(LAGS) - HALF) % PLEN) / PLEN
    inverse = np.zeros((2 * NF, 512))
    inverse[:NF, :LAGS] = np.cos(phases)
    inverse[NF:, :LAGS] = -np.sin(phases)
    low = ml_dtypes.bfloat16
    return full.astype(low), half.astype(low), twiddle, inverse.astype(low)


def flip(index, bit):
    return index + bit - 2 * bit * lax.rem(lax.div(index, bit), 2)


def exchange_kernel(
    traces, assign, matching, quad, quad_assign, near, near_assign,
    pair, pair_assign, relay, relay_assign, sems, ready,
):
    g, b = lax.axis_index("group"), lax.axis_index("blk")
    core, x, high = lax.rem(b, 2), lax.rem(lax.div(b, 2), 4), lax.rem(lax.div(b, 8), 2)
    left, right = lax.rem(b + 63, 64), lax.rem(b + 1, 64)
    last = jnp.logical_and(x == 3, core == 1)
    first = jnp.logical_and(x == 0, core == 0)
    below = high == 0
    far = g >= 4
    up_out = jnp.logical_and(last, below)
    up_in = jnp.logical_and(first, high == 1)
    up_low = jnp.logical_and(up_out, g < 4)
    up_high = jnp.logical_and(up_out, far)
    relay_low = up_high
    relay_high = jnp.logical_and(jnp.logical_and(last, high == 1), g < 4)
    in_low = jnp.logical_and(up_in, g < 4)
    in_high = jnp.logical_and(up_in, far)
    plain_out = jnp.logical_not(up_out)
    plain_in = jnp.logical_not(up_in)

    g4, g1, g2 = flip(g, 4), flip(g, 1), flip(g, 2)
    g3 = flip(g1, 2)

    def copies(base, source, source_assign, target, target_assign, device):
        return [
            pltpu.make_async_remote_copy(
                a, t, sems.at[base + 2 * i], sems.at[base + 2 * i + 1], device_id=device, device_id_type=MESH
            )
            for i, (a, t) in enumerate(((source, target), (source_assign, target_assign)))
        ]

    def start(cs):
        for c in cs:
            c.start()

    def wait_recv(cs):
        for c in cs:
            c.wait_recv()

    def wait_send(cs):
        for c in cs:
            c.wait_send()

    barrier = pltpu.get_barrier_semaphore()

    def greet(device):
        pl.semaphore_signal(barrier, inc=1, device_id=device, device_id_type=MESH)

    for peer in (g4, g3, g2, g1):
        greet((peer, b))
    @pl.when(plain_in)
    def _():
        greet((g, left))

    @pl.when(in_low)
    def _():
        greet((g + 4, left))

    @pl.when(in_high)
    def _():
        greet((g - 4, left + 8))

    @pl.when(up_high)
    def _():
        greet((g - 4, b + 8))

    own = pltpu.make_async_copy(traces, pair.at[0], sems.at[20])
    own_assign = pltpu.make_async_copy(assign, pair_assign.at[0], sems.at[21])
    own.start()
    own_assign.start()

    count = 4 + plain_out.astype(jnp.int32) + relay_low.astype(jnp.int32) + 2 * relay_high.astype(jnp.int32)
    pl.semaphore_wait(barrier, count)

    @pl.when(relay_high)
    def _():
        pl.semaphore_signal(ready, inc=1, device_id=(lax.rem(g + 4, 8), lax.rem(b + 56, 64)), device_id_type=MESH)

    to_near = copies(0, traces, assign, near, near_assign, (g, right))

    @pl.when(plain_out)
    def _():
        start(to_near)

    to_pair = copies(4, traces, assign, pair.at[1], pair_assign.at[1], (g4, b))
    start(to_pair)
    own.wait()
    own_assign.wait()
    wait_recv(to_pair)

    pass_low = copies(0, pair.at[1], pair_assign.at[1], near, near_assign, (lax.rem(g + 4, 8), right))

    @pl.when(relay_low)
    def _():
        start(pass_low)

    round_ = matching[0, 0]
    bit = lax.rem(lax.div(round_, 4), 2)
    quad[0] = pair[bit]
    quad_assign[0] = pair_assign[bit]
    to_quad = [
        copies(4 + 4 * i, quad.at[0], quad_assign.at[0], quad.at[i], quad_assign.at[i], (peer, b))
        for i, peer in ((3, g3), (2, g2), (1, g1))
    ]
    for cs in to_quad:
        start(cs)

    to_relay = copies(22, traces, assign, relay, relay_assign, (lax.rem(g + 4, 8), lax.rem(b + 8, 64)))

    @pl.when(up_high)
    def _():
        pl.semaphore_wait(ready, 1)
        start(to_relay)

    pass_high = copies(26, relay, relay_assign, near, near_assign, (lax.rem(g + 4, 8), lax.rem(b + 57, 64)))

    @pl.when(relay_high)
    def _():
        wait_recv(to_relay)
        start(pass_high)

    for cs in to_quad:
        wait_recv(cs)

    @pl.when(jnp.logical_not(in_high))
    def _():
        wait_recv(to_near)

    @pl.when(in_high)
    def _():
        wait_recv(pass_high)

    wait_send(to_pair)
    for cs in to_quad:
        wait_send(cs)

    @pl.when(plain_out)
    def _():
        wait_send(to_near)

    @pl.when(relay_low)
    def _():
        wait_send(pass_low)

    @pl.when(up_high)
    def _():
        wait_send(to_relay)

    @pl.when(relay_high)
    def _():
        wait_send(pass_high)


def correlate_kernel(
    traces, assign, quad, quad_assign, near, near_assign, matching, full, half, twiddle, inverse,
    between, within, samples, real, imag, cross,
):
    samples[:, 1152:1280] = jnp.zeros((72, 128), f32)
    slot = lax.rem(matching[0, 0], 4)
    for r in range(4):
        mine, other, beside = assign[0, r], quad_assign[slot, r], near_assign[0, r]
        for comp in range(3):
            a = traces[r, comp].astype(f32)
            p = quad[slot, r, comp].astype(f32)
            n = near[r, comp].astype(f32)
            for w in range(2):
                samples[pl.ds(12 * w + 3 * mine + comp, 1), 0:NSAMP] = a[w : w + 1]
                samples[pl.ds(24 + 24 * w + 4 * comp + other, 1), 0:NSAMP] = p[w : w + 1]
                samples[pl.ds(36 + 24 * w + 4 * comp + beside, 1), 0:NSAMP] = n[w : w + 1]
    v = [samples[:, FAST * i : FAST * i + FAST] for i in range(5)]
    energy = v[0] * v[0]
    for i in range(1, 5):
        energy = energy + v[i] * v[i]
    scale = lax.rsqrt(jnp.sum(energy, axis=-1, keepdims=True) * (1.0 / NSAMP) + EPSILON)
    even, odd = v[0] + v[2] + v[4], v[1] + v[3]
    minus, plus = v[0] - v[3], v[0] + v[3]
    parts = (
        (minus + 0.5 * (v[1] - v[2] - v[4]), -ROOT3 * (v[1] + v[2] - v[4])),
        (plus - 0.5 * (v[1] + v[2] + v[4]), -ROOT3 * (v[1] - v[2] + v[4])),
        (even - odd, None),
        (even + odd, None),
    )
    column = 0
    for i, (re, im) in enumerate(parts):
        c = jnp.tile(twiddle[16 * i : 16 * i + 8, :], (9, 1))
        s = jnp.tile(twiddle[16 * i + 8 : 16 * i + 16, :], (9, 1))
        if im is None:
            re, im = re * c, -re * s
        else:
            re, im = re * c + im * s, im * c - re * s
        turned = jnp.concatenate([re.astype(bf16), im.astype(bf16)], axis=1)
        count = FIRSTS[i][1]
        table = full if count == FAST else half
        spectra = jnp.dot(turned, table[...], preferred_element_type=f32)
        real[:, column : column + count] = spectra[:, :count] * scale
        imag[:, column : column + count] = spectra[:, count:] * scale
        column += count
    for q in range(6):
        lanes = slice(128 * q, 128 * q + 128)
        right = [(real[24 + 24 * w : 48 + 24 * w, lanes], imag[24 + 24 * w : 48 + 24 * w, lanes]) for w in range(2)]
        for two in range(6):
            reals, imags = [], []
            for row in (2 * two, 2 * two + 1):
                re = im = None
                for w in range(2):
                    at = 12 * w + row
                    left_re = jnp.broadcast_to(real[at : at + 1, lanes], (24, 128))
                    left_im = jnp.broadcast_to(imag[at : at + 1, lanes], (24, 128))
                    right_re, right_im = right[w]
                    a = left_re * right_re + left_im * right_im
                    d = left_re * right_im - left_im * right_re
                    re, im = (a, d) if re is None else (re + a, im + d)
                reals.append(re)
                imags.append(im)
            rows = slice(48 * two, 48 * two + 48)
            cross[rows, 128 * q : 128 * q + 128] = jnp.concatenate(reals, 0).astype(bf16)
            cross[rows, NF + 128 * q : NF + 128 * q + 128] = jnp.concatenate(imags, 0).astype(bf16)
    lags = jnp.dot(cross[...], inverse[...], preferred_element_type=f32) * SCALE
    for row in range(12):
        for comp in range(3):
            at = 24 * row + 4 * comp
            between[row // 3, row % 3, comp] = lags[at : at + 4, :LAGS].astype(bf16)
            within[row // 3, row % 3, comp] = lags[at + 12 : at + 16, :LAGS].astype(bf16)


def shards(traces, assign, matching):
    vmem = pl.BlockSpec(memory_space=pltpu.VMEM)
    smem = pl.BlockSpec(memory_space=pltpu.SMEM)
    anywhere = pl.BlockSpec(memory_space=pl.ANY)
    block = traces.shape
    assign = assign.reshape(1, 4)
    quad, quad_assign, near, near_assign = pl.pallas_call(
        exchange_kernel,
        out_shape=(
            jax.ShapeDtypeStruct((4,) + block, bf16),
            jax.ShapeDtypeStruct((4, 1, 4), jnp.int32),
            jax.ShapeDtypeStruct(block, bf16),
            jax.ShapeDtypeStruct((1, 4), jnp.int32),
        ),
        in_specs=[anywhere, anywhere, smem],
        out_specs=(vmem, vmem, vmem, vmem),
        scratch_shapes=[
            pltpu.VMEM((2,) + block, bf16),
            pltpu.VMEM((2, 1, 4), jnp.int32),
            pltpu.VMEM(block, bf16),
            pltpu.VMEM((1, 4), jnp.int32),
            pltpu.SemaphoreType.DMA((30,)),
            pltpu.SemaphoreType.REGULAR,
        ],
        compiler_params=pltpu.CompilerParams(collective_id=0, has_side_effects=True),
        name="exchange",
    )(traces, assign, matching)
    full, half, twiddle, inverse = (jnp.asarray(t) for t in tables())
    between, within = pl.pallas_call(
        correlate_kernel,
        out_shape=(jax.ShapeDtypeStruct((4, 3, 3, 4, LAGS), bf16),) * 2,
        in_specs=[vmem, smem, vmem, smem, vmem, smem, smem, vmem, vmem, vmem, vmem],
        out_specs=(vmem, vmem),
        scratch_shapes=[
            pltpu.VMEM((72, 1280), f32),
            pltpu.VMEM((72, NF), f32),
            pltpu.VMEM((72, NF), f32),
            pltpu.VMEM((288, 2 * NF), bf16),
        ],
        cost_estimate=pl.CostEstimate(flops=600_000_000, bytes_accessed=3_000_000, transcendentals=0),
        name="correlate",
    )(traces, assign, quad, quad_assign.reshape(4, 4), near, near_assign, matching, full, half, twiddle, inverse)
    return tuple(jnp.transpose(v, (0, 3, 1, 2, 4)) for v in (between, within))


def solution(mesh):
    placed = (P(("group", "blk"), None, None, None), P(("group", "blk")), P("blk", None))
    return jax.shard_map(
        shards,
        mesh=mesh,
        in_specs=placed,
        out_specs=(
            P(("group", "blk"), None, None, None, None),
            P(("group", "blk"), None, None, None, None),
        ),
        check_vma=False,
    )
```

```python
import functools
import math

import jax
import jax.numpy as jnp
import ml_dtypes
import numpy as np
from jax import lax
from jax.experimental import pallas as pl
from jax.experimental.pallas import tpu as pltpu
from jax.sharding import PartitionSpec as P

WIN = 2
NSAMP = 1200
PLEN = 1536
NF = 768
HALF = 200
LAGS = 401
FAST = 256
EPSILON = 1e-05
SCALE = 2.0 / (PLEN * math.sqrt(NSAMP * WIN))
ROOT3 = math.sqrt(3) / 2
MESH = pl.DeviceIdType.MESH
bf16, f32 = jnp.bfloat16, jnp.float32

FIRSTS = ((1, 256), (2, 256), (3, 128), (6, 128))
BINS = np.concatenate([first + 6 * np.arange(count) for first, count in FIRSTS])


def tables():
    n = np.arange(FAST)
    phases = 2 * np.pi * (np.outer(n, n) % FAST) / FAST
    c, s = np.cos(phases), np.sin(phases)
    full = np.block([[c, -s], [s, c]])
    half = np.concatenate([full[:, :128], full[:, 256:384]], axis=1)
    twiddle = np.zeros((64, FAST), np.float32)
    for i, (first, _) in enumerate(FIRSTS):
        phases = 2 * np.pi * n * first / PLEN
        twiddle[16 * i : 16 * i + 8] = np.cos(phases)
        twiddle[16 * i + 8 : 16 * i + 16] = np.sin(phases)
    phases = 2 * np.pi * (np.outer(BINS, np.arange(LAGS) - HALF) % PLEN) / PLEN
    inverse = np.zeros((2 * NF, 512))
    inverse[:NF, :LAGS] = np.cos(phases)
    inverse[NF:, :LAGS] = -np.sin(phases)
    low = ml_dtypes.bfloat16
    return full.astype(low), half.astype(low), twiddle, inverse.astype(low)


def flip(index, bit):
    return index + bit - 2 * bit * lax.rem(lax.div(index, bit), 2)


def exchange_kernel(
    traces, assign, matching, quad, quad_assign, near, near_assign,
    pair, pair_assign, sems, ready,
):
    g, b = lax.axis_index("group"), lax.axis_index("blk")
    core, x, high = lax.rem(b, 2), lax.rem(lax.div(b, 2), 4), lax.rem(lax.div(b, 8), 2)
    left, right = lax.rem(b + 63, 64), lax.rem(b + 1, 64)
    last = jnp.logical_and(x == 3, core == 1)
    first = jnp.logical_and(x == 0, core == 0)
    below, above = high == 0, high == 1
    up_out = jnp.logical_and(last, below)
    up_in = jnp.logical_and(first, above)
    near_half = g < 4
    far_half = g >= 4
    plain_out = jnp.logical_not(up_out)
    plain_in = jnp.logical_not(up_in)
    opposite = lax.rem(g + 4, 8)

    g4, g1, g2 = flip(g, 4), flip(g, 1), flip(g, 2)
    g3 = flip(g1, 2)

    def copies(base, source, source_assign, target, target_assign, device):
        return [
            pltpu.make_async_remote_copy(
                a, t, sems.at[base + 2 * i], sems.at[base + 2 * i + 1], device_id=device, device_id_type=MESH
            )
            for i, (a, t) in enumerate(((source, target), (source_assign, target_assign)))
        ]

    def start(cs):
        for c in cs:
            c.start()

    def wait_recv(cs):
        for c in cs:
            c.wait_recv()

    def wait_send(cs):
        for c in cs:
            c.wait_send()

    barrier = pltpu.get_barrier_semaphore()

    def one(flag):
        return flag.astype(jnp.int32)

    def greet(device):
        pl.semaphore_signal(barrier, inc=1, device_id=device, device_id_type=MESH)

    def tell(i, device):
        pl.semaphore_signal(ready.at[i], inc=1, device_id=device, device_id_type=MESH)

    peers = (g4, g1, g2, g3)
    ordered = jnp.logical_or(below, last)
    mutual = jnp.logical_not(ordered)
    witness = jnp.logical_and(up_in, near_half)
    count = one(plain_out) + 2 * one(witness)
    for peer in peers:
        count = count + one(jnp.logical_or(mutual, peer < g))

        @pl.when(jnp.logical_or(mutual, peer > g))
        def _():
            greet((peer, b))

    @pl.when(plain_in)
    def _():
        greet((g, left))

    @pl.when(jnp.logical_and(up_out, near_half))
    def _():
        greet((g, right))

    @pl.when(jnp.logical_and(up_out, far_half))
    def _():
        greet((opposite, right))

    own = pltpu.make_async_copy(traces, pair.at[0], sems.at[20])
    own_assign = pltpu.make_async_copy(assign, pair_assign.at[0], sems.at[21])
    own.start()
    own_assign.start()

    @pl.when(count > 0)
    def _():
        pl.semaphore_wait(barrier, count)

    to_near = copies(0, traces, assign, near, near_assign, (g, right))

    @pl.when(plain_out)
    def _():
        start(to_near)

    for i, peer in enumerate(peers):

        @pl.when(jnp.logical_and(ordered, peer < g))
        def _():
            tell(i, (peer, b))

    @pl.when(witness)
    def _():
        tell(4, (g, left))
        tell(4, (opposite, left))

    def wait_ready(i):
        @pl.when(jnp.logical_and(ordered, peers[i] > g))
        def _():
            pl.semaphore_wait(ready.at[i], 1)

    to_pair = copies(4, traces, assign, pair.at[1], pair_assign.at[1], (g4, b))
    wait_ready(0)
    start(to_pair)

    def step_up():
        pl.semaphore_wait(ready.at[4], 1)
        start(to_near)

    pl.when(jnp.logical_and(up_out, far_half))(step_up)
    own.wait()
    own_assign.wait()
    wait_recv(to_pair)

    round_ = matching[0, 0]
    bit = lax.rem(lax.div(round_, 4), 2)
    quad[0] = pair[bit]
    quad_assign[0] = pair_assign[bit]
    to_quad = []
    for i in (2, 3, 1):
        to_quad.append(copies(4 + 4 * i, quad.at[0], quad_assign.at[0], quad.at[i], quad_assign.at[i], (peers[i], b)))
        wait_ready(i)
        start(to_quad[-1])

    pl.when(jnp.logical_and(up_out, near_half))(step_up)

    for cs in to_quad:
        wait_recv(cs)
    wait_recv(to_near)
    wait_send(to_pair)
    for cs in to_quad:
        wait_send(cs)
    wait_send(to_near)


def correlate_kernel(
    traces, assign, quad, quad_assign, near, near_assign, matching, full, half, twiddle, inverse,
    between, within, samples, real, imag, cross,
):
    samples[:, 1152:1280] = jnp.zeros((72, 128), f32)
    slot = lax.rem(matching[0, 0], 4)
    for r in range(4):
        mine, other, beside = assign[0, r], quad_assign[slot, r], near_assign[0, r]
        for comp in range(3):
            a = traces[r, comp].astype(f32)
            p = quad[slot, r, comp].astype(f32)
            n = near[r, comp].astype(f32)
            for w in range(2):
                samples[pl.ds(12 * w + 3 * mine + comp, 1), 0:NSAMP] = a[w : w + 1]
                samples[pl.ds(24 + 24 * w + 4 * comp + other, 1), 0:NSAMP] = p[w : w + 1]
                samples[pl.ds(36 + 24 * w + 4 * comp + beside, 1), 0:NSAMP] = n[w : w + 1]
    v = [samples[:, FAST * i : FAST * i + FAST] for i in range(5)]
    energy = v[0] * v[0]
    for i in range(1, 5):
        energy = energy + v[i] * v[i]
    scale = lax.rsqrt(jnp.sum(energy, axis=-1, keepdims=True) * (1.0 / NSAMP) + EPSILON)
    even, odd = v[0] + v[2] + v[4], v[1] + v[3]
    minus, plus = v[0] - v[3], v[0] + v[3]
    parts = (
        (minus + 0.5 * (v[1] - v[2] - v[4]), -ROOT3 * (v[1] + v[2] - v[4])),
        (plus - 0.5 * (v[1] + v[2] + v[4]), -ROOT3 * (v[1] - v[2] + v[4])),
        (even - odd, None),
        (even + odd, None),
    )
    column = 0
    for i, (re, im) in enumerate(parts):
        c = jnp.tile(twiddle[16 * i : 16 * i + 8, :], (9, 1))
        s = jnp.tile(twiddle[16 * i + 8 : 16 * i + 16, :], (9, 1))
        if im is None:
            re, im = re * c, -re * s
        else:
            re, im = re * c + im * s, im * c - re * s
        turned = jnp.concatenate([re.astype(bf16), im.astype(bf16)], axis=1)
        count = FIRSTS[i][1]
        table = full if count == FAST else half
        spectra = jnp.dot(turned, table[...], preferred_element_type=f32)
        real[:, column : column + count] = spectra[:, :count] * scale
        imag[:, column : column + count] = spectra[:, count:] * scale
        column += count
    for q in range(6):
        lanes = slice(128 * q, 128 * q + 128)
        right = [(real[24 + 24 * w : 48 + 24 * w, lanes], imag[24 + 24 * w : 48 + 24 * w, lanes]) for w in range(2)]
        for two in range(6):
            reals, imags = [], []
            for row in (2 * two, 2 * two + 1):
                re = im = None
                for w in range(2):
                    at = 12 * w + row
                    left_re = jnp.broadcast_to(real[at : at + 1, lanes], (24, 128))
                    left_im = jnp.broadcast_to(imag[at : at + 1, lanes], (24, 128))
                    right_re, right_im = right[w]
                    a = left_re * right_re + left_im * right_im
                    d = left_re * right_im - left_im * right_re
                    re, im = (a, d) if re is None else (re + a, im + d)
                reals.append(re)
                imags.append(im)
            rows = slice(48 * two, 48 * two + 48)
            cross[rows, 128 * q : 128 * q + 128] = jnp.concatenate(reals, 0).astype(bf16)
            cross[rows, NF + 128 * q : NF + 128 * q + 128] = jnp.concatenate(imags, 0).astype(bf16)
    lags = jnp.dot(cross[...], inverse[...], preferred_element_type=f32) * SCALE
    for row in range(12):
        for comp in range(3):
            at = 24 * row + 4 * comp
            between[row // 3, row % 3, comp] = lags[at : at + 4, :LAGS].astype(bf16)
            within[row // 3, row % 3, comp] = lags[at + 12 : at + 16, :LAGS].astype(bf16)


def shards(traces, assign, matching):
    vmem = pl.BlockSpec(memory_space=pltpu.VMEM)
    smem = pl.BlockSpec(memory_space=pltpu.SMEM)
    anywhere = pl.BlockSpec(memory_space=pl.ANY)
    block = traces.shape
    assign = assign.reshape(1, 4)
    quad, quad_assign, near, near_assign = pl.pallas_call(
        exchange_kernel,
        out_shape=(
            jax.ShapeDtypeStruct((4,) + block, bf16),
            jax.ShapeDtypeStruct((4, 1, 4), jnp.int32),
            jax.ShapeDtypeStruct(block, bf16),
            jax.ShapeDtypeStruct((1, 4), jnp.int32),
        ),
        in_specs=[anywhere, anywhere, smem],
        out_specs=(vmem, vmem, vmem, vmem),
        scratch_shapes=[
            pltpu.VMEM((2,) + block, bf16),
            pltpu.VMEM((2, 1, 4), jnp.int32),
            pltpu.SemaphoreType.DMA((22,)),
            pltpu.SemaphoreType.REGULAR((5,)),
        ],
        compiler_params=pltpu.CompilerParams(collective_id=0, has_side_effects=True),
        name="exchange",
    )(traces, assign, matching)
    full, half, twiddle, inverse = (jnp.asarray(t) for t in tables())
    between, within = pl.pallas_call(
        correlate_kernel,
        out_shape=(jax.ShapeDtypeStruct((4, 3, 3, 4, LAGS), bf16),) * 2,
        in_specs=[vmem, smem, vmem, smem, vmem, smem, smem, vmem, vmem, vmem, vmem],
        out_specs=(vmem, vmem),
        scratch_shapes=[
            pltpu.VMEM((72, 1280), f32),
            pltpu.VMEM((72, NF), f32),
            pltpu.VMEM((72, NF), f32),
            pltpu.VMEM((288, 2 * NF), bf16),
        ],
        cost_estimate=pl.CostEstimate(flops=600_000_000, bytes_accessed=3_000_000, transcendentals=0),
        name="correlate",
    )(traces, assign, quad, quad_assign.reshape(4, 4), near, near_assign, matching, full, half, twiddle, inverse)
    return tuple(jnp.transpose(v, (0, 3, 1, 2, 4)) for v in (between, within))


def solution(mesh):
    placed = (P(("group", "blk"), None, None, None), P(("group", "blk")), P("blk", None))
    return jax.shard_map(
        shards,
        mesh=mesh,
        in_specs=placed,
        out_specs=(
            P(("group", "blk"), None, None, None, None),
            P(("group", "blk"), None, None, None, None),
        ),
        check_vma=False,
    )
```

```python
import functools
import math

import jax
import jax.numpy as jnp
import ml_dtypes
import numpy as np
from jax import lax
from jax.experimental import pallas as pl
from jax.experimental.pallas import tpu as pltpu
from jax.sharding import PartitionSpec as P

WIN = 2
NSAMP = 1200
PLEN = 1536
NF = 768
HALF = 200
LAGS = 401
FAST = 256
EPSILON = 1e-05
SCALE = 2.0 / (PLEN * math.sqrt(NSAMP * WIN))
ROOT3 = math.sqrt(3) / 2
MESH = pl.DeviceIdType.MESH
bf16, f32 = jnp.bfloat16, jnp.float32

FIRSTS = ((1, 256), (2, 256), (3, 128), (6, 128))
BINS = np.concatenate([first + 6 * np.arange(count) for first, count in FIRSTS])


def tables():
    n = np.arange(FAST)
    phases = 2 * np.pi * (np.outer(n, n) % FAST) / FAST
    c, s = np.cos(phases), np.sin(phases)
    full = np.block([[c, -s], [s, c]])
    half = np.concatenate([full[:, :128], full[:, 256:384]], axis=1)
    twiddle = np.zeros((64, FAST), np.float32)
    for i, (first, _) in enumerate(FIRSTS):
        phases = 2 * np.pi * n * first / PLEN
        twiddle[16 * i : 16 * i + 8] = np.cos(phases)
        twiddle[16 * i + 8 : 16 * i + 16] = np.sin(phases)
    phases = 2 * np.pi * (np.outer(BINS, np.arange(LAGS) - HALF) % PLEN) / PLEN
    inverse = np.zeros((2 * NF, 512))
    inverse[:NF, :LAGS] = np.cos(phases)
    inverse[NF:, :LAGS] = -np.sin(phases)
    low = ml_dtypes.bfloat16
    return full.astype(low), half.astype(low), twiddle, inverse.astype(low)


def flip(index, bit):
    return index + bit - 2 * bit * lax.rem(lax.div(index, bit), 2)


def inverse_order(assign):
    rows = [assign(r) for r in range(4)]
    order = []
    for s in range(4):
        found = 0
        for r in range(1, 4):
            found = jnp.where(rows[r] == s, r, found)
        order.append(found)
    return order


def load_samples(samples, block, order, row):
    for station in range(4):
        for comp in range(3):
            both = block(order[station], comp).astype(f32)
            for w in range(2):
                at = 16 * w + row(station, comp)
                samples[at : at + 1, 0:NSAMP] = both[w : w + 1]


def transform(samples, full, half, twiddle, real, imag):
    v = [samples[:, FAST * i : FAST * i + FAST] for i in range(5)]
    energy = v[0] * v[0]
    for i in range(1, 5):
        energy = energy + v[i] * v[i]
    scale = lax.rsqrt(jnp.sum(energy, axis=-1, keepdims=True) * (1.0 / NSAMP) + EPSILON)
    even, odd = v[0] + v[2] + v[4], v[1] + v[3]
    minus, plus = v[0] - v[3], v[0] + v[3]
    parts = (
        (minus + 0.5 * (v[1] - v[2] - v[4]), -ROOT3 * (v[1] + v[2] - v[4])),
        (plus - 0.5 * (v[1] + v[2] + v[4]), -ROOT3 * (v[1] - v[2] + v[4])),
        (even - odd, None),
        (even + odd, None),
    )
    turned = []
    for i, (re, im) in enumerate(parts):
        c = jnp.tile(twiddle[16 * i : 16 * i + 8, :], (4, 1))
        s = jnp.tile(twiddle[16 * i + 8 : 16 * i + 16, :], (4, 1))
        if im is None:
            re, im = re * c, -re * s
        else:
            re, im = re * c + im * s, im * c - re * s
        turned.append(jnp.concatenate([re.astype(bf16), im.astype(bf16)], axis=1))
    column = 0
    for i, table, count in ((0, full, FAST), (2, half, 128)):
        both = jnp.concatenate(turned[i : i + 2], axis=0)
        spectra = jnp.dot(both, table[...], preferred_element_type=f32)
        for k in range(2):
            real[:, column : column + count] = spectra[32 * k : 32 * k + 32, :count] * scale
            imag[:, column : column + count] = spectra[32 * k : 32 * k + 32, count:] * scale
            column += count


def multiply(left, right, cross):
    for q in range(3):
        lanes = slice(256 * q, 256 * q + 256)
        other = [[part[16 * w : 16 * w + 16, lanes] for part in right] for w in range(2)]
        for row in range(12):
            re = im = None
            for w in range(2):
                at = 16 * w + row
                left_re = jnp.broadcast_to(left[0][at : at + 1, lanes], (16, 256))
                left_im = jnp.broadcast_to(left[1][at : at + 1, lanes], (16, 256))
                right_re, right_im = other[w]
                a = left_re * right_re + left_im * right_im
                d = left_re * right_im - left_im * right_re
                re, im = (a, d) if re is None else (re + a, im + d)
            cross[16 * row : 16 * row + 16, lanes] = re.astype(bf16)
            cross[16 * row : 16 * row + 16, NF + 256 * q : NF + 256 * q + 256] = im.astype(bf16)


def correlate_kernel(
    traces, assign, matching_hbm, full_hbm, half_hbm, twiddle_hbm, inverse_hbm,
    between, within,
    own, pair, quad, near, matching, own_assign, pair_assign, quad_assign, near_assign,
    full, half, twiddle, inverse, samples, left_re, left_im, right_re, right_im, cross, lags,
    sems, local, ready,
):
    g, b = lax.axis_index("group"), lax.axis_index("blk")
    core, x, high = lax.rem(b, 2), lax.rem(lax.div(b, 2), 4), lax.rem(lax.div(b, 8), 2)
    left, right = lax.rem(b + 63, 64), lax.rem(b + 1, 64)
    last = jnp.logical_and(x == 3, core == 1)
    first = jnp.logical_and(x == 0, core == 0)
    below, above = high == 0, high == 1
    up_out = jnp.logical_and(last, below)
    up_in = jnp.logical_and(first, above)
    near_half = g < 4
    far_half = g >= 4
    plain_out = jnp.logical_not(up_out)
    plain_in = jnp.logical_not(up_in)
    opposite = lax.rem(g + 4, 8)

    g4, g1, g2 = flip(g, 4), flip(g, 1), flip(g, 2)
    g3 = flip(g1, 2)

    def copies(base, source, source_assign, target, target_assign, device):
        return [
            pltpu.make_async_remote_copy(
                a, t, sems.at[base + 2 * i], sems.at[base + 2 * i + 1], device_id=device, device_id_type=MESH
            )
            for i, (a, t) in enumerate(((source, target), (source_assign, target_assign)))
        ]

    def start(cs):
        for c in cs:
            c.start()

    def wait_recv(cs):
        for c in cs:
            c.wait_recv()

    def wait_send(cs):
        for c in cs:
            c.wait_send()

    barrier = pltpu.get_barrier_semaphore()

    def one(flag):
        return flag.astype(jnp.int32)

    def greet(device):
        pl.semaphore_signal(barrier, inc=1, device_id=device, device_id_type=MESH)

    def tell(i, device):
        pl.semaphore_signal(ready.at[i], inc=1, device_id=device, device_id_type=MESH)

    peers = (g4, g1, g2, g3)
    ordered = jnp.logical_or(below, last)
    mutual = jnp.logical_not(ordered)
    witness = jnp.logical_and(up_in, near_half)
    count = one(plain_out) + 2 * one(witness)
    for peer in peers:
        count = count + one(jnp.logical_or(mutual, peer < g))

        @pl.when(jnp.logical_or(mutual, peer > g))
        def _():
            greet((peer, b))

    @pl.when(plain_in)
    def _():
        greet((g, left))

    @pl.when(jnp.logical_and(up_out, near_half))
    def _():
        greet((g, right))

    @pl.when(jnp.logical_and(up_out, far_half))
    def _():
        greet((opposite, right))

    arrivals = [
        pltpu.make_async_copy(source, target, local.at[i])
        for i, (source, target) in enumerate(
            (
                (traces, own),
                (traces, pair.at[0]),
                (assign, pair_assign.at[0]),
                (assign, own_assign),
                (matching_hbm, matching),
                (full_hbm, full),
                (half_hbm, half),
                (twiddle_hbm, twiddle),
                (inverse_hbm, inverse),
            )
        )
    ]
    for c in arrivals:
        c.start()

    @pl.when(count > 0)
    def _():
        pl.semaphore_wait(barrier, count)

    to_near = copies(0, traces, assign, near, near_assign, (g, right))

    @pl.when(plain_out)
    def _():
        start(to_near)

    for i, peer in enumerate(peers):

        @pl.when(jnp.logical_and(ordered, peer < g))
        def _():
            tell(i, (peer, b))

    @pl.when(witness)
    def _():
        tell(4, (g, left))
        tell(4, (opposite, left))

    def wait_ready(i):
        @pl.when(jnp.logical_and(ordered, peers[i] > g))
        def _():
            pl.semaphore_wait(ready.at[i], 1)

    to_pair = copies(4, traces, assign, pair.at[1], pair_assign.at[1], (g4, b))
    wait_ready(0)
    start(to_pair)

    def step_up():
        pl.semaphore_wait(ready.at[4], 1)
        start(to_near)

    pl.when(jnp.logical_and(up_out, far_half))(step_up)
    samples[...] = jnp.zeros(samples.shape, f32)
    for c in arrivals:
        c.wait()
    order = inverse_order(lambda r: own_assign[0, r])
    load_samples(samples, lambda r, comp: own[r, comp], order, lambda station, comp: 3 * station + comp)
    transform(samples, full, half, twiddle, left_re, left_im)
    wait_recv(to_pair)

    round_ = matching[0, 0]
    bit = lax.rem(lax.div(round_, 4), 2)
    quad[0] = pair[bit]
    for r in range(4):
        quad_assign[0, 0, r] = pair_assign[bit, 0, r]
    to_quad = []
    for i in (2, 3, 1):
        to_quad.append(copies(4 + 4 * i, quad.at[0], quad_assign.at[0], quad.at[i], quad_assign.at[i], (peers[i], b)))
        wait_ready(i)
        start(to_quad[-1])

    pl.when(jnp.logical_and(up_out, near_half))(step_up)

    samples[...] = jnp.zeros(samples.shape, f32)
    slot = lax.rem(round_, 4)
    results = [pltpu.make_async_copy(lags.at[k], out, local.at[9 + k]) for k, out in enumerate((within, between))]

    def other_row(station, comp):
        return 4 * comp + station

    def side(step, carry):
        which = step + one(first) - 2 * step * one(first)

        @pl.when(which == 0)
        def _():
            wait_recv(to_near)
            order = inverse_order(lambda r: near_assign[0, r])
            load_samples(samples, lambda r, comp: near[r, comp], order, other_row)

        @pl.when(which == 1)
        def _():
            for cs in to_quad:
                wait_recv(cs)
            order = inverse_order(lambda r: quad_assign[slot, 0, r])
            load_samples(samples, lambda r, comp: quad[slot, r, comp], order, other_row)

        transform(samples, full, half, twiddle, right_re, right_im)
        multiply((left_re, left_im), (right_re, right_im), cross)
        result = jnp.dot(cross[...], inverse[...], preferred_element_type=f32) * SCALE
        for row in range(12):
            for comp in range(3):
                at = 16 * row + 4 * comp
                lags[which, row // 3, row % 3, comp] = result[at : at + 4, :LAGS].astype(bf16)
        for k in range(2):
            pl.when(which == k)(results[k].start)
        return carry

    lax.fori_loop(0, 2, side, 0)
    wait_send(to_pair)
    for cs in to_quad:
        wait_send(cs)
    wait_send(to_near)
    for c in results:
        c.wait()


def shards(traces, assign, matching):
    anywhere = pl.BlockSpec(memory_space=pl.ANY)
    hbm = pl.BlockSpec(memory_space=pltpu.HBM)
    block = traces.shape
    assign = assign.reshape(1, 4)
    tables_ = [jnp.asarray(t) for t in tables()]
    result = (4, 3, 3, 4, LAGS)
    between, within = pl.pallas_call(
        correlate_kernel,
        out_shape=(jax.ShapeDtypeStruct(result, bf16),) * 2,
        in_specs=[hbm] * 7,
        out_specs=(anywhere, anywhere),
        scratch_shapes=[
            pltpu.VMEM(block, bf16),
            pltpu.VMEM((2,) + block, bf16),
            pltpu.VMEM((4,) + block, bf16),
            pltpu.VMEM(block, bf16),
            pltpu.SMEM(matching.shape, jnp.int32),
            pltpu.SMEM((1, 4), jnp.int32),
            pltpu.SMEM((2, 1, 4), jnp.int32),
            pltpu.SMEM((4, 1, 4), jnp.int32),
            pltpu.SMEM((1, 4), jnp.int32),
            *(pltpu.VMEM(t.shape, t.dtype) for t in tables_),
            pltpu.VMEM((32, 1280), f32),
            *(pltpu.VMEM((32, NF), f32) for _ in range(4)),
            pltpu.VMEM((192, 2 * NF), bf16),
            pltpu.VMEM((2,) + result, bf16),
            pltpu.SemaphoreType.DMA((20,)),
            pltpu.SemaphoreType.DMA((11,)),
            pltpu.SemaphoreType.REGULAR((5,)),
        ],
        compiler_params=pltpu.CompilerParams(collective_id=0, has_side_effects=True, vmem_limit_bytes=32 << 20),
        name="correlate",
    )(*(pltpu.with_memory_space_constraint(v, pltpu.HBM) for v in (traces, assign, matching, *tables_)))
    return tuple(jnp.transpose(v, (0, 3, 1, 2, 4)) for v in (between, within))


def solution(mesh):
    placed = (P(("group", "blk"), None, None, None), P(("group", "blk")), P("blk", None))
    return jax.shard_map(
        shards,
        mesh=mesh,
        in_specs=placed,
        out_specs=(
            P(("group", "blk"), None, None, None, None),
            P(("group", "blk"), None, None, None, None),
        ),
        check_vma=False,
    )
```

```python
import functools
import math

import jax
import jax.numpy as jnp
import ml_dtypes
import numpy as np
from jax import lax
from jax.experimental import pallas as pl
from jax.experimental.pallas import tpu as pltpu
from jax.sharding import PartitionSpec as P

WIN = 2
NSAMP = 1200
PLEN = 1536
NF = 768
HALF = 200
LAGS = 401
FAST = 256
EPSILON = 1e-05
SCALE = 2.0 / (PLEN * math.sqrt(NSAMP * WIN))
ROOT3 = math.sqrt(3) / 2
MESH = pl.DeviceIdType.MESH
bf16, f32 = jnp.bfloat16, jnp.float32

FIRSTS = ((1, 256), (2, 256), (3, 128), (6, 128))
BINS = np.concatenate([first + 6 * np.arange(count) for first, count in FIRSTS])


def tables():
    n = np.arange(FAST)
    phases = 2 * np.pi * (np.outer(n, n) % FAST) / FAST
    c, s = np.cos(phases), np.sin(phases)
    full = np.block([[c, -s], [s, c]])
    half = np.concatenate([full[:, :128], full[:, 256:384]], axis=1)
    twiddle = np.zeros((64, FAST), np.float32)
    for i, (first, _) in enumerate(FIRSTS):
        phases = 2 * np.pi * n * first / PLEN
        twiddle[16 * i : 16 * i + 8] = np.cos(phases)
        twiddle[16 * i + 8 : 16 * i + 16] = np.sin(phases)
    phases = 2 * np.pi * (np.outer(BINS, np.arange(LAGS) - HALF) % PLEN) / PLEN
    inverse = np.zeros((2 * NF, 512))
    inverse[:NF, :LAGS] = np.cos(phases)
    inverse[NF:, :LAGS] = -np.sin(phases)
    low = ml_dtypes.bfloat16
    return full.astype(low), half.astype(low), twiddle, inverse.astype(low)


def flip(index, bit):
    return index + bit - 2 * bit * lax.rem(lax.div(index, bit), 2)


def inverse_order(assign):
    rows = [assign(r) for r in range(4)]
    order = []
    for s in range(4):
        found = 0
        for r in range(1, 4):
            found = jnp.where(rows[r] == s, r, found)
        order.append(found)
    return order


def load_samples(samples, block, order, row):
    for station in range(4):
        for comp in range(3):
            both = block(order[station], comp).astype(f32)
            for w in range(2):
                at = 16 * w + row(station, comp)
                samples[at : at + 1, 0:NSAMP] = both[w : w + 1]


def transform(samples, full, half, twiddle, real, imag):
    v = [samples[:, FAST * i : FAST * i + FAST] for i in range(5)]
    energy = v[0] * v[0]
    for i in range(1, 5):
        energy = energy + v[i] * v[i]
    scale = lax.rsqrt(jnp.sum(energy, axis=-1, keepdims=True) * (1.0 / NSAMP) + EPSILON)
    even, odd = v[0] + v[2] + v[4], v[1] + v[3]
    minus, plus = v[0] - v[3], v[0] + v[3]
    parts = (
        (minus + 0.5 * (v[1] - v[2] - v[4]), -ROOT3 * (v[1] + v[2] - v[4])),
        (plus - 0.5 * (v[1] + v[2] + v[4]), -ROOT3 * (v[1] - v[2] + v[4])),
        (even - odd, None),
        (even + odd, None),
    )
    turned = []
    for i, (re, im) in enumerate(parts):
        c = jnp.tile(twiddle[16 * i : 16 * i + 8, :], (4, 1))
        s = jnp.tile(twiddle[16 * i + 8 : 16 * i + 16, :], (4, 1))
        if im is None:
            re, im = re * c, -re * s
        else:
            re, im = re * c + im * s, im * c - re * s
        turned.append(jnp.concatenate([re.astype(bf16), im.astype(bf16)], axis=1))
    column = 0
    for i, table, count in ((0, full, FAST), (2, half, 128)):
        both = jnp.concatenate(turned[i : i + 2], axis=0)
        spectra = jnp.dot(both, table[...], preferred_element_type=f32)
        for k in range(2):
            real[:, column : column + count] = spectra[32 * k : 32 * k + 32, :count] * scale
            imag[:, column : column + count] = spectra[32 * k : 32 * k + 32, count:] * scale
            column += count


def multiply(left, right, cross):
    for q in range(3):
        lanes = slice(256 * q, 256 * q + 256)
        other = [[part[16 * w : 16 * w + 16, lanes] for part in right] for w in range(2)]
        for row in range(12):
            re = im = None
            for w in range(2):
                at = 16 * w + row
                left_re = jnp.broadcast_to(left[0][at : at + 1, lanes], (16, 256))
                left_im = jnp.broadcast_to(left[1][at : at + 1, lanes], (16, 256))
                right_re, right_im = other[w]
                a = left_re * right_re + left_im * right_im
                d = left_re * right_im - left_im * right_re
                re, im = (a, d) if re is None else (re + a, im + d)
            cross[16 * row : 16 * row + 16, lanes] = re.astype(bf16)
            cross[16 * row : 16 * row + 16, NF + 256 * q : NF + 256 * q + 256] = im.astype(bf16)


def exclusive_or(a, b):
    a1, b1 = lax.div(a, 2), lax.div(b, 2)
    a0, b0 = a - 2 * a1, b - 2 * b1
    return 2 * (a1 + b1 - 2 * a1 * b1) + a0 + b0 - 2 * a0 * b0


def correlate_kernel(
    traces, assign, matching_hbm, full_hbm, half_hbm, twiddle_hbm, inverse_hbm,
    out,
    own, pair, quad, near, matching, own_assign, pair_assign, quad_assign, near_assign,
    full, half, twiddle, inverse, samples, left_re, left_im, right_re, right_im, cross, lags,
    sems, local, ready,
):
    g, b = lax.axis_index("group"), lax.axis_index("blk")
    core, x, high = lax.rem(b, 2), lax.rem(lax.div(b, 2), 4), lax.rem(lax.div(b, 8), 2)
    left, right = lax.rem(b + 63, 64), lax.rem(b + 1, 64)
    last = jnp.logical_and(x == 3, core == 1)
    first = jnp.logical_and(x == 0, core == 0)
    below, above = high == 0, high == 1
    up_out = jnp.logical_and(last, below)
    up_in = jnp.logical_and(first, above)
    near_half = g < 4
    far_half = g >= 4
    plain_out = jnp.logical_not(up_out)
    plain_in = jnp.logical_not(up_in)
    opposite = lax.rem(g + 4, 8)

    g4, g1, g2 = flip(g, 4), flip(g, 1), flip(g, 2)
    g3 = flip(g1, 2)

    def copies(base, source, source_assign, target, target_assign, device):
        return [
            pltpu.make_async_remote_copy(
                a, t, sems.at[base + 2 * i], sems.at[base + 2 * i + 1], device_id=device, device_id_type=MESH
            )
            for i, (a, t) in enumerate(((source, target), (source_assign, target_assign)))
        ]

    def start(cs):
        for c in cs:
            c.start()

    def wait_recv(cs):
        for c in cs:
            c.wait_recv()

    def wait_send(cs):
        for c in cs:
            c.wait_send()

    barrier = pltpu.get_barrier_semaphore()

    def one(flag):
        return flag.astype(jnp.int32)

    def greet(device):
        pl.semaphore_signal(barrier, inc=1, device_id=device, device_id_type=MESH)

    def tell(i, device):
        pl.semaphore_signal(ready.at[i], inc=1, device_id=device, device_id_type=MESH)

    peers = (g4, g1, g2, g3)
    ordered = jnp.logical_or(below, last)
    mutual = jnp.logical_not(ordered)
    witness = jnp.logical_and(up_in, near_half)
    count = one(plain_out) + 2 * one(witness)
    for peer in peers:
        count = count + one(jnp.logical_or(mutual, peer < g))

        @pl.when(jnp.logical_or(mutual, peer > g))
        def _():
            greet((peer, b))

    @pl.when(plain_in)
    def _():
        greet((g, left))

    @pl.when(jnp.logical_and(up_out, near_half))
    def _():
        greet((g, right))

    @pl.when(jnp.logical_and(up_out, far_half))
    def _():
        greet((opposite, right))

    arrivals = [
        pltpu.make_async_copy(source, target, local.at[i])
        for i, (source, target) in enumerate(
            (
                (traces, own),
                (traces, pair.at[0]),
                (assign, pair_assign.at[0]),
                (assign, own_assign),
                (matching_hbm, matching),
                (full_hbm, full),
                (half_hbm, half),
                (twiddle_hbm, twiddle),
                (inverse_hbm, inverse),
            )
        )
    ]
    for c in arrivals:
        c.start()

    @pl.when(count > 0)
    def _():
        pl.semaphore_wait(barrier, count)

    to_near = copies(0, traces, assign, near, near_assign, (g, right))

    @pl.when(plain_out)
    def _():
        start(to_near)

    for i, peer in enumerate(peers):

        @pl.when(jnp.logical_and(ordered, peer < g))
        def _():
            tell(i, (peer, b))

    @pl.when(witness)
    def _():
        tell(4, (g, left))
        tell(4, (opposite, left))

    def wait_ready(i):
        @pl.when(jnp.logical_and(ordered, peers[i] > g))
        def _():
            pl.semaphore_wait(ready.at[i], 1)

    to_pair = copies(4, traces, assign, pair.at[1], pair_assign.at[1], (g4, b))
    wait_ready(0)
    start(to_pair)

    def step_up():
        pl.semaphore_wait(ready.at[4], 1)
        start(to_near)

    pl.when(jnp.logical_and(up_out, far_half))(step_up)
    samples[...] = jnp.zeros(samples.shape, f32)
    for c in arrivals:
        c.wait()
    order = inverse_order(lambda r: own_assign[0, r])
    load_samples(samples, lambda r, comp: own[r, comp], order, lambda station, comp: 3 * station + comp)
    transform(samples, full, half, twiddle, left_re, left_im)
    wait_recv(to_pair)

    round_ = matching[0, 0]
    bit = lax.rem(lax.div(round_, 4), 2)
    quad[0] = pair[bit]
    for r in range(4):
        quad_assign[0, 0, r] = pair_assign[bit, 0, r]
    place = lax.rem(g, 4)
    to_quad = []
    for k in range(3):
        target = k + one(place <= k)
        i = exclusive_or(place, target)
        peer = g - place + target
        cs = copies(4 + 4 * i, quad.at[0], quad_assign.at[0], quad.at[i], quad_assign.at[i], (peer, b))

        @pl.when(jnp.logical_and(ordered, peer > g))
        def _():
            pl.semaphore_wait(ready.at[i], 1)

        start(cs)
        to_quad.append(cs)
        if k == 0:

            @pl.when(below)
            def _():
                wait_send(cs)

    from_quad = [
        copies(4 + 4 * i, quad.at[0], quad_assign.at[0], quad.at[i], quad_assign.at[i], (peers[i], b))
        for i in range(1, 4)
    ]

    pl.when(jnp.logical_and(up_out, near_half))(step_up)

    samples[...] = jnp.zeros(samples.shape, f32)
    slot = lax.rem(round_, 4)
    results = [pltpu.make_async_copy(lags.at[k], out.at[k], local.at[9 + k]) for k in range(2)]

    def other_row(station, comp):
        return 4 * comp + station

    def side(step, carry):
        which = step + one(first) - 2 * step * one(first)

        @pl.when(which == 0)
        def _():
            wait_recv(to_near)
            order = inverse_order(lambda r: near_assign[0, r])
            load_samples(samples, lambda r, comp: near[r, comp], order, other_row)

        @pl.when(which == 1)
        def _():
            for cs in from_quad:
                wait_recv(cs)
            order = inverse_order(lambda r: quad_assign[slot, 0, r])
            load_samples(samples, lambda r, comp: quad[slot, r, comp], order, other_row)

        transform(samples, full, half, twiddle, right_re, right_im)
        multiply((left_re, left_im), (right_re, right_im), cross)
        result = jnp.dot(cross[...], inverse[...], preferred_element_type=f32) * SCALE
        for row in range(12):
            for comp in range(3):
                at = 16 * row + 4 * comp
                lags[which, row // 3, row % 3, comp] = result[at : at + 4, :LAGS].astype(bf16)
        for k in range(2):
            pl.when(which == k)(results[k].start)
        return carry

    lax.fori_loop(0, 2, side, 0)
    wait_send(to_pair)
    pl.when(above)(lambda: wait_send(to_quad[0]))
    for cs in to_quad[1:]:
        wait_send(cs)
    wait_send(to_near)
    for c in results:
        c.wait()


def shards(traces, assign, matching):
    anywhere = pl.BlockSpec(memory_space=pl.ANY)
    hbm = pl.BlockSpec(memory_space=pltpu.HBM)
    block = traces.shape
    assign = assign.reshape(1, 4)
    tables_ = [jnp.asarray(t) for t in tables()]
    result = (2, 4, 3, 3, 4, LAGS)
    both = pl.pallas_call(
        correlate_kernel,
        out_shape=jax.ShapeDtypeStruct(result, bf16),
        in_specs=[hbm] * 7,
        out_specs=anywhere,
        scratch_shapes=[
            pltpu.VMEM(block, bf16),
            pltpu.VMEM((2,) + block, bf16),
            pltpu.VMEM((4,) + block, bf16),
            pltpu.VMEM(block, bf16),
            pltpu.SMEM(matching.shape, jnp.int32),
            pltpu.SMEM((1, 4), jnp.int32),
            pltpu.SMEM((2, 1, 4), jnp.int32),
            pltpu.SMEM((4, 1, 4), jnp.int32),
            pltpu.SMEM((1, 4), jnp.int32),
            *(pltpu.VMEM(t.shape, t.dtype) for t in tables_),
            pltpu.VMEM((32, 1280), f32),
            *(pltpu.VMEM((32, NF), f32) for _ in range(4)),
            pltpu.VMEM((192, 2 * NF), bf16),
            pltpu.VMEM(result, bf16),
            pltpu.SemaphoreType.DMA((20,)),
            pltpu.SemaphoreType.DMA((11,)),
            pltpu.SemaphoreType.REGULAR((5,)),
        ],
        compiler_params=pltpu.CompilerParams(collective_id=0, has_side_effects=True, vmem_limit_bytes=32 << 20),
        name="correlate",
    )(*(pltpu.with_memory_space_constraint(v, pltpu.HBM) for v in (traces, assign, matching, *tables_)))
    return tuple(jnp.transpose(v, (0, 3, 1, 2, 4)) for v in (both[1], both[0]))


def solution(mesh):
    placed = (P(("group", "blk"), None, None, None), P(("group", "blk")), P("blk", None))
    return jax.shard_map(
        shards,
        mesh=mesh,
        in_specs=placed,
        out_specs=(
            P(("group", "blk"), None, None, None, None),
            P(("group", "blk"), None, None, None, None),
        ),
        check_vma=False,
    )
```

```python
import functools
import math

import jax
import jax.numpy as jnp
import ml_dtypes
import numpy as np
from jax import lax
from jax.experimental import pallas as pl
from jax.experimental.pallas import tpu as pltpu
from jax.sharding import PartitionSpec as P

WIN = 2
NSAMP = 1200
PLEN = 1536
NF = 768
HALF = 200
LAGS = 401
FAST = 256
EPSILON = 1e-05
SCALE = 2.0 / (PLEN * math.sqrt(NSAMP * WIN))
ROOT3 = math.sqrt(3) / 2
MESH = pl.DeviceIdType.MESH
bf16, f32 = jnp.bfloat16, jnp.float32

FIRSTS = ((1, 256), (2, 256), (3, 128), (6, 128))
BINS = np.concatenate([first + 6 * np.arange(count) for first, count in FIRSTS])


def tables():
    n = np.arange(FAST)
    phases = 2 * np.pi * (np.outer(n, n) % FAST) / FAST
    c, s = np.cos(phases), np.sin(phases)
    full = np.block([[c, -s], [s, c]])
    half = np.concatenate([full[:, :128], full[:, 256:384]], axis=1)
    twiddle = np.zeros((64, FAST), np.float32)
    for i, (first, _) in enumerate(FIRSTS):
        phases = 2 * np.pi * n * first / PLEN
        twiddle[16 * i : 16 * i + 8] = np.cos(phases)
        twiddle[16 * i + 8 : 16 * i + 16] = np.sin(phases)
    phases = 2 * np.pi * (np.outer(BINS, np.arange(LAGS) - HALF) % PLEN) / PLEN
    inverse = np.zeros((2 * NF, 512))
    inverse[:NF, :LAGS] = np.cos(phases)
    inverse[NF:, :LAGS] = -np.sin(phases)
    low = ml_dtypes.bfloat16
    return full.astype(low), half.astype(low), twiddle, inverse.astype(low)


def flip(index, bit):
    return index + bit - 2 * bit * lax.rem(lax.div(index, bit), 2)


def inverse_order(assign):
    rows = [assign(r) for r in range(4)]
    order = []
    for s in range(4):
        found = 0
        for r in range(1, 4):
            found = jnp.where(rows[r] == s, r, found)
        order.append(found)
    return order


def load_samples(samples, block, order, row):
    for station in range(4):
        for comp in range(3):
            both = block(order[station], comp).astype(f32)
            for w in range(2):
                at = 16 * w + row(station, comp)
                samples[at : at + 1, 0:NSAMP] = both[w : w + 1]


def transform(samples, full, half, twiddle, real, imag):
    v = [samples[:, FAST * i : FAST * i + FAST] for i in range(5)]
    energy = v[0] * v[0]
    for i in range(1, 5):
        energy = energy + v[i] * v[i]
    scale = lax.rsqrt(jnp.sum(energy, axis=-1, keepdims=True) * (1.0 / NSAMP) + EPSILON)
    even, odd = v[0] + v[2] + v[4], v[1] + v[3]
    minus, plus = v[0] - v[3], v[0] + v[3]
    parts = (
        (minus + 0.5 * (v[1] - v[2] - v[4]), -ROOT3 * (v[1] + v[2] - v[4])),
        (plus - 0.5 * (v[1] + v[2] + v[4]), -ROOT3 * (v[1] - v[2] + v[4])),
        (even - odd, None),
        (even + odd, None),
    )
    turned = []
    for i, (re, im) in enumerate(parts):
        c = jnp.tile(twiddle[16 * i : 16 * i + 8, :], (4, 1))
        s = jnp.tile(twiddle[16 * i + 8 : 16 * i + 16, :], (4, 1))
        if im is None:
            re, im = re * c, -re * s
        else:
            re, im = re * c + im * s, im * c - re * s
        turned.append(jnp.concatenate([re.astype(bf16), im.astype(bf16)], axis=1))
    column = 0
    for i, table, count in ((0, full, FAST), (2, half, 128)):
        both = jnp.concatenate(turned[i : i + 2], axis=0)
        spectra = jnp.dot(both, table[...], preferred_element_type=f32)
        for k in range(2):
            real[:, column : column + count] = spectra[32 * k : 32 * k + 32, :count] * scale
            imag[:, column : column + count] = spectra[32 * k : 32 * k + 32, count:] * scale
            column += count


def multiply(left, right, cross):
    for q in range(3):
        lanes = slice(256 * q, 256 * q + 256)
        other = [[part[16 * w : 16 * w + 16, lanes] for part in right] for w in range(2)]
        for row in range(12):
            re = im = None
            for w in range(2):
                at = 16 * w + row
                left_re = jnp.broadcast_to(left[0][at : at + 1, lanes], (16, 256))
                left_im = jnp.broadcast_to(left[1][at : at + 1, lanes], (16, 256))
                right_re, right_im = other[w]
                a = left_re * right_re + left_im * right_im
                d = left_re * right_im - left_im * right_re
                re, im = (a, d) if re is None else (re + a, im + d)
            cross[16 * row : 16 * row + 16, lanes] = re.astype(bf16)
            cross[16 * row : 16 * row + 16, NF + 256 * q : NF + 256 * q + 256] = im.astype(bf16)


def exclusive_or(a, b):
    a1, b1 = lax.div(a, 2), lax.div(b, 2)
    a0, b0 = a - 2 * a1, b - 2 * b1
    return 2 * (a1 + b1 - 2 * a1 * b1) + a0 + b0 - 2 * a0 * b0


def correlate_kernel(
    traces, assign, matching_hbm, full_hbm, half_hbm, twiddle_hbm, inverse_hbm,
    out,
    own, pair, quad, near, matching, own_assign, pair_assign, quad_assign, near_assign,
    full, half, twiddle, inverse, samples, left_re, left_im, right_re, right_im, cross,
    sems, local, ready,
):
    g, b = lax.axis_index("group"), lax.axis_index("blk")
    core, x, high = lax.rem(b, 2), lax.rem(lax.div(b, 2), 4), lax.rem(lax.div(b, 8), 2)
    left, right = lax.rem(b + 63, 64), lax.rem(b + 1, 64)
    last = jnp.logical_and(x == 3, core == 1)
    first = jnp.logical_and(x == 0, core == 0)
    below, above = high == 0, high == 1
    up_out = jnp.logical_and(last, below)
    up_in = jnp.logical_and(first, above)
    near_half = g < 4
    far_half = g >= 4
    plain_out = jnp.logical_not(up_out)
    plain_in = jnp.logical_not(up_in)
    opposite = lax.rem(g + 4, 8)

    g4, g1, g2 = flip(g, 4), flip(g, 1), flip(g, 2)
    g3 = flip(g1, 2)

    def copies(base, source, source_assign, target, target_assign, device):
        return [
            pltpu.make_async_remote_copy(
                a, t, sems.at[base + 2 * i], sems.at[base + 2 * i + 1], device_id=device, device_id_type=MESH
            )
            for i, (a, t) in enumerate(((source, target), (source_assign, target_assign)))
        ]

    def start(cs):
        for c in cs:
            c.start()

    def wait_recv(cs):
        for c in cs:
            c.wait_recv()

    def wait_send(cs):
        for c in cs:
            c.wait_send()

    barrier = pltpu.get_barrier_semaphore()

    def one(flag):
        return flag.astype(jnp.int32)

    def greet(device):
        pl.semaphore_signal(barrier, inc=1, device_id=device, device_id_type=MESH)

    def tell(i, device):
        pl.semaphore_signal(ready.at[i], inc=1, device_id=device, device_id_type=MESH)

    peers = (g4, g1, g2, g3)
    ordered = jnp.logical_or(below, last)
    mutual = jnp.logical_not(ordered)
    witness = jnp.logical_and(up_in, near_half)
    count = one(plain_out) + 2 * one(witness)
    source = jnp.logical_and(jnp.logical_and(above, last), near_half)
    count = count + 3 * one(jnp.logical_and(jnp.logical_and(above, last), far_half))
    settled = jnp.logical_not(source)
    for peer in peers:
        count = count + one(jnp.logical_and(settled, jnp.logical_or(mutual, peer < g)))

        @pl.when(jnp.logical_and(settled, jnp.logical_or(mutual, peer > g)))
        def _():
            greet((peer, b))

    @pl.when(source)
    def _():
        for other in range(4, 8):
            greet((other, b))

    @pl.when(plain_in)
    def _():
        greet((g, left))

    @pl.when(jnp.logical_and(up_out, near_half))
    def _():
        greet((g, right))

    @pl.when(jnp.logical_and(up_out, far_half))
    def _():
        greet((opposite, right))

    arrivals = [
        pltpu.make_async_copy(source, target, local.at[i])
        for i, (source, target) in enumerate(
            (
                (traces, own),
                (traces, pair.at[0]),
                (assign, pair_assign.at[0]),
                (assign, own_assign),
                (matching_hbm, matching),
                (full_hbm, full),
                (half_hbm, half),
                (twiddle_hbm, twiddle),
                (inverse_hbm, inverse),
            )
        )
    ]
    for c in arrivals:
        c.start()

    @pl.when(count > 0)
    def _():
        pl.semaphore_wait(barrier, count)

    to_near = copies(0, traces, assign, near, near_assign, (g, right))

    @pl.when(plain_out)
    def _():
        start(to_near)

    for i, peer in enumerate(peers):

        @pl.when(jnp.logical_and(jnp.logical_and(ordered, settled), peer < g))
        def _():
            tell(i, (peer, b))

    @pl.when(witness)
    def _():
        tell(4, (g, left))
        tell(4, (opposite, left))

    def wait_ready(i):
        @pl.when(jnp.logical_and(ordered, peers[i] > g))
        def _():
            pl.semaphore_wait(ready.at[i], 1)

    to_pair = copies(4, traces, assign, pair.at[1], pair_assign.at[1], (g4, b))
    wait_ready(0)
    start(to_pair)

    def step_up():
        pl.semaphore_wait(ready.at[4], 1)
        start(to_near)

    pl.when(jnp.logical_and(up_out, far_half))(step_up)
    samples[...] = jnp.zeros(samples.shape, f32)
    for c in arrivals:
        c.wait()
    order = inverse_order(lambda r: own_assign[0, r])
    load_samples(samples, lambda r, comp: own[r, comp], order, lambda station, comp: 3 * station + comp)
    transform(samples, full, half, twiddle, left_re, left_im)
    wait_recv(to_pair)

    round_ = matching[0, 0]
    bit = lax.rem(lax.div(round_, 4), 2)
    quad[0] = pair[bit]
    for r in range(4):
        quad_assign[0, 0, r] = pair_assign[bit, 0, r]
    place = lax.rem(g, 4)
    to_quad = []
    for k in range(3):
        target = k + one(place <= k)
        i = exclusive_or(place, target)
        peer = g - place + target
        cs = copies(4 + 4 * i, quad.at[0], quad_assign.at[0], quad.at[i], quad_assign.at[i], (peer, b))

        @pl.when(jnp.logical_and(jnp.logical_and(ordered, settled), peer > g))
        def _():
            pl.semaphore_wait(ready.at[i], 1)

        start(cs)
        to_quad.append(cs)
        if k == 0:

            @pl.when(below)
            def _():
                wait_send(cs)

    from_quad = [
        copies(4 + 4 * i, quad.at[0], quad_assign.at[0], quad.at[i], quad_assign.at[i], (peers[i], b))
        for i in range(1, 4)
    ]

    pl.when(jnp.logical_and(up_out, near_half))(step_up)

    samples[...] = jnp.zeros(samples.shape, f32)
    slot = lax.rem(round_, 4)

    def other_row(station, comp):
        return 4 * comp + station

    def side(step, carry):
        which = exclusive_or(step, one(jnp.logical_and(first, near_half)))

        @pl.when(which == 0)
        def _():
            wait_recv(to_near)
            order = inverse_order(lambda r: near_assign[0, r])
            load_samples(samples, lambda r, comp: near[r, comp], order, other_row)

        @pl.when(which == 1)
        def _():
            for cs in from_quad:
                wait_recv(cs)
            order = inverse_order(lambda r: quad_assign[slot, 0, r])
            load_samples(samples, lambda r, comp: quad[slot, r, comp], order, other_row)

        transform(samples, full, half, twiddle, right_re, right_im)
        multiply((left_re, left_im), (right_re, right_im), cross)
        result = jnp.dot(cross[...], inverse[...], preferred_element_type=f32) * SCALE
        for row in range(12):
            for comp in range(3):
                at = 16 * row + 4 * comp
                out[which, row // 3, row % 3, comp] = result[at : at + 4, :LAGS].astype(bf16)
        return carry

    lax.fori_loop(0, 2, side, 0)
    wait_send(to_pair)
    pl.when(above)(lambda: wait_send(to_quad[0]))
    for cs in to_quad[1:]:
        wait_send(cs)
    wait_send(to_near)


def place_kernel(both, within, between, sems):
    copies = [pltpu.make_async_copy(both.at[k], out, sems.at[k]) for k, out in enumerate((within, between))]
    for c in copies:
        c.start()
    for c in copies:
        c.wait()


def shards(traces, assign, matching):
    anywhere = pl.BlockSpec(memory_space=pl.ANY)
    hbm = pl.BlockSpec(memory_space=pltpu.HBM)
    block = traces.shape
    assign = assign.reshape(1, 4)
    tables_ = [jnp.asarray(t) for t in tables()]
    result = (2, 4, 3, 3, 4, LAGS)
    both = pl.pallas_call(
        correlate_kernel,
        out_shape=jax.ShapeDtypeStruct(result, bf16),
        in_specs=[hbm] * 7,
        out_specs=pl.BlockSpec(memory_space=pltpu.VMEM),
        scratch_shapes=[
            pltpu.VMEM(block, bf16),
            pltpu.VMEM((2,) + block, bf16),
            pltpu.VMEM((4,) + block, bf16),
            pltpu.VMEM(block, bf16),
            pltpu.SMEM(matching.shape, jnp.int32),
            pltpu.SMEM((1, 4), jnp.int32),
            pltpu.SMEM((2, 1, 4), jnp.int32),
            pltpu.SMEM((4, 1, 4), jnp.int32),
            pltpu.SMEM((1, 4), jnp.int32),
            *(pltpu.VMEM(t.shape, t.dtype) for t in tables_),
            pltpu.VMEM((32, 1280), f32),
            *(pltpu.VMEM((32, NF), f32) for _ in range(4)),
            pltpu.VMEM((192, 2 * NF), bf16),
            pltpu.SemaphoreType.DMA((20,)),
            pltpu.SemaphoreType.DMA((11,)),
            pltpu.SemaphoreType.REGULAR((5,)),
        ],
        compiler_params=pltpu.CompilerParams(collective_id=0, has_side_effects=True, vmem_limit_bytes=32 << 20),
        name="correlate",
    )(*(pltpu.with_memory_space_constraint(v, pltpu.HBM) for v in (traces, assign, matching, *tables_)))
    within, between = pl.pallas_call(
        place_kernel,
        out_shape=(jax.ShapeDtypeStruct(result[1:], bf16),) * 2,
        in_specs=[anywhere],
        out_specs=(anywhere, anywhere),
        scratch_shapes=[pltpu.SemaphoreType.DMA((2,))],
        compiler_params=pltpu.CompilerParams(vmem_limit_bytes=16 << 20),
        name="place",
    )(both)
    return tuple(jnp.transpose(v, (0, 3, 1, 2, 4)) for v in (between, within))


def solution(mesh):
    placed = (P(("group", "blk"), None, None, None), P(("group", "blk")), P("blk", None))
    return jax.shard_map(
        shards,
        mesh=mesh,
        in_specs=placed,
        out_specs=(
            P(("group", "blk"), None, None, None, None),
            P(("group", "blk"), None, None, None, None),
        ),
        check_vma=False,
    )
```

```python
import functools
import math

import jax
import jax.numpy as jnp
import ml_dtypes
import numpy as np
from jax import lax
from jax.experimental import pallas as pl
from jax.experimental.pallas import tpu as pltpu
from jax.sharding import PartitionSpec as P

WIN = 2
NSAMP = 1200
PLEN = 1536
NF = 768
HALF = 200
LAGS = 401
FAST = 256
EPSILON = 1e-05
SCALE = 2.0 / (PLEN * math.sqrt(NSAMP * WIN))
ROOT3 = math.sqrt(3) / 2
MESH = pl.DeviceIdType.MESH
bf16, f32 = jnp.bfloat16, jnp.float32

FIRSTS = ((1, 256), (2, 256), (3, 128), (6, 128))
BINS = np.concatenate([first + 6 * np.arange(count) for first, count in FIRSTS])


def tables():
    n = np.arange(FAST)
    phases = 2 * np.pi * (np.outer(n, n) % FAST) / FAST
    c, s = np.cos(phases), np.sin(phases)
    full = np.block([[c, -s], [s, c]])
    half = np.concatenate([full[:, :128], full[:, 256:384]], axis=1)
    twiddle = np.zeros((64, FAST), np.float32)
    for i, (first, _) in enumerate(FIRSTS):
        phases = 2 * np.pi * n * first / PLEN
        twiddle[16 * i : 16 * i + 8] = np.cos(phases)
        twiddle[16 * i + 8 : 16 * i + 16] = np.sin(phases)
    phases = 2 * np.pi * (np.outer(BINS, np.arange(LAGS) - HALF) % PLEN) / PLEN
    inverse = np.zeros((2 * NF, 512))
    inverse[:NF, :LAGS] = np.cos(phases)
    inverse[NF:, :LAGS] = -np.sin(phases)
    low = ml_dtypes.bfloat16
    return full.astype(low), half.astype(low), twiddle, inverse.astype(low)


def flip(index, bit):
    return index + bit - 2 * bit * lax.rem(lax.div(index, bit), 2)


def inverse_order(assign):
    rows = [assign(r) for r in range(4)]
    order = []
    for s in range(4):
        found = 0
        for r in range(1, 4):
            found = jnp.where(rows[r] == s, r, found)
        order.append(found)
    return order


def load_samples(samples, block, order, row):
    for station in range(4):
        for comp in range(3):
            both = block(order[station], comp).astype(f32)
            for w in range(2):
                at = 16 * w + row(station, comp)
                samples[at : at + 1, 0:NSAMP] = both[w : w + 1]


def transform(samples, full, half, twiddle, real, imag):
    v = [samples[:, FAST * i : FAST * i + FAST] for i in range(5)]
    energy = v[0] * v[0]
    for i in range(1, 5):
        energy = energy + v[i] * v[i]
    scale = lax.rsqrt(jnp.sum(energy, axis=-1, keepdims=True) * (1.0 / NSAMP) + EPSILON)
    even, odd = v[0] + v[2] + v[4], v[1] + v[3]
    minus, plus = v[0] - v[3], v[0] + v[3]
    parts = (
        (minus + 0.5 * (v[1] - v[2] - v[4]), -ROOT3 * (v[1] + v[2] - v[4])),
        (plus - 0.5 * (v[1] + v[2] + v[4]), -ROOT3 * (v[1] - v[2] + v[4])),
        (even - odd, None),
        (even + odd, None),
    )
    turned = []
    for i, (re, im) in enumerate(parts):
        c = jnp.tile(twiddle[16 * i : 16 * i + 8, :], (4, 1))
        s = jnp.tile(twiddle[16 * i + 8 : 16 * i + 16, :], (4, 1))
        if im is None:
            re, im = re * c, -re * s
        else:
            re, im = re * c + im * s, im * c - re * s
        turned.append(jnp.concatenate([re.astype(bf16), im.astype(bf16)], axis=1))
    column = 0
    for i, table, count in ((0, full, FAST), (2, half, 128)):
        both = jnp.concatenate(turned[i : i + 2], axis=0)
        spectra = jnp.dot(both, table[...], preferred_element_type=f32)
        for k in range(2):
            real[:, column : column + count] = spectra[32 * k : 32 * k + 32, :count] * scale
            imag[:, column : column + count] = spectra[32 * k : 32 * k + 32, count:] * scale
            column += count


def multiply(left, right, cross):
    for q in range(3):
        lanes = slice(256 * q, 256 * q + 256)
        other = [[part[16 * w : 16 * w + 16, lanes] for part in right] for w in range(2)]
        for row in range(12):
            re = im = None
            for w in range(2):
                at = 16 * w + row
                left_re = jnp.broadcast_to(left[0][at : at + 1, lanes], (16, 256))
                left_im = jnp.broadcast_to(left[1][at : at + 1, lanes], (16, 256))
                right_re, right_im = other[w]
                a = left_re * right_re + left_im * right_im
                d = left_re * right_im - left_im * right_re
                re, im = (a, d) if re is None else (re + a, im + d)
            cross[16 * row : 16 * row + 16, lanes] = re.astype(bf16)
            cross[16 * row : 16 * row + 16, NF + 256 * q : NF + 256 * q + 256] = im.astype(bf16)


def exclusive_or(a, b):
    a1, b1 = lax.div(a, 2), lax.div(b, 2)
    a0, b0 = a - 2 * a1, b - 2 * b1
    return 2 * (a1 + b1 - 2 * a1 * b1) + a0 + b0 - 2 * a0 * b0


def correlate_kernel(
    traces, assign, matching_hbm, full_hbm, half_hbm, twiddle_hbm, inverse_hbm,
    out,
    own, pair, quad, near, matching, own_assign, pair_assign, quad_assign, near_assign,
    full, half, twiddle, inverse, samples, left_re, left_im, right_re, right_im, cross,
    sems, local, ready,
):
    g, b = lax.axis_index("group"), lax.axis_index("blk")
    core, x, high = lax.rem(b, 2), lax.rem(lax.div(b, 2), 4), lax.rem(lax.div(b, 8), 2)
    left, right = lax.rem(b + 63, 64), lax.rem(b + 1, 64)
    last = jnp.logical_and(x == 3, core == 1)
    first = jnp.logical_and(x == 0, core == 0)
    below, above = high == 0, high == 1
    up_out = jnp.logical_and(last, below)
    up_in = jnp.logical_and(first, above)
    near_half = g < 4
    far_half = g >= 4
    plain_out = jnp.logical_not(up_out)
    plain_in = jnp.logical_not(up_in)
    opposite = lax.rem(g + 4, 8)

    g4, g1, g2 = flip(g, 4), flip(g, 1), flip(g, 2)
    g3 = flip(g1, 2)

    def copies(base, source, source_assign, target, target_assign, device):
        return [
            pltpu.make_async_remote_copy(
                a, t, sems.at[base + 2 * i], sems.at[base + 2 * i + 1], device_id=device, device_id_type=MESH
            )
            for i, (a, t) in enumerate(((source, target), (source_assign, target_assign)))
        ]

    def start(cs):
        for c in cs:
            c.start()

    def wait_recv(cs):
        for c in cs:
            c.wait_recv()

    def wait_send(cs):
        for c in cs:
            c.wait_send()

    barrier = pltpu.get_barrier_semaphore()

    def one(flag):
        return flag.astype(jnp.int32)

    def greet(device):
        pl.semaphore_signal(barrier, inc=1, device_id=device, device_id_type=MESH)

    def tell(i, device):
        pl.semaphore_signal(ready.at[i], inc=1, device_id=device, device_id_type=MESH)

    peers = (g4, g1, g2, g3)
    ordered = jnp.logical_or(below, last)
    mutual = jnp.logical_not(ordered)
    witness = jnp.logical_and(up_in, near_half)
    count = one(plain_out) + 2 * one(witness)
    source = jnp.logical_and(jnp.logical_and(above, last), near_half)
    count = count + 3 * one(jnp.logical_and(jnp.logical_and(above, last), far_half))
    settled = jnp.logical_not(source)
    for peer in peers:
        count = count + one(jnp.logical_and(settled, jnp.logical_or(mutual, peer < g)))

        @pl.when(jnp.logical_and(settled, jnp.logical_or(mutual, peer > g)))
        def _():
            greet((peer, b))

    @pl.when(source)
    def _():
        for other in range(4, 8):
            greet((other, b))

    @pl.when(plain_in)
    def _():
        greet((g, left))

    @pl.when(jnp.logical_and(up_out, near_half))
    def _():
        greet((g, right))

    @pl.when(jnp.logical_and(up_out, far_half))
    def _():
        greet((opposite, right))

    arrivals = [
        pltpu.make_async_copy(source, target, local.at[i])
        for i, (source, target) in enumerate(
            (
                (traces, own),
                (traces, pair.at[0]),
                (assign, pair_assign.at[0]),
                (assign, own_assign),
                (matching_hbm, matching),
                (full_hbm, full),
                (half_hbm, half),
                (twiddle_hbm, twiddle),
                (inverse_hbm, inverse),
            )
        )
    ]
    for c in arrivals:
        c.start()

    @pl.when(count > 0)
    def _():
        pl.semaphore_wait(barrier, count)

    to_near = copies(0, traces, assign, near, near_assign, (g, right))

    @pl.when(plain_out)
    def _():
        start(to_near)

    for i, peer in enumerate(peers):

        @pl.when(jnp.logical_and(jnp.logical_and(ordered, settled), peer < g))
        def _():
            tell(i, (peer, b))

    @pl.when(witness)
    def _():
        tell(4, (g, left))
        tell(4, (opposite, left))

    def wait_ready(i):
        @pl.when(jnp.logical_and(ordered, peers[i] > g))
        def _():
            pl.semaphore_wait(ready.at[i], 1)

    def halves(base, source, source_assign, target, target_assign, device):
        parts = (
            (source.at[pl.ds(0, 2)], target.at[pl.ds(0, 2)]),
            (source_assign, target_assign),
            (source.at[pl.ds(2, 2)], target.at[pl.ds(2, 2)]),
        )
        cs = [
            pltpu.make_async_remote_copy(
                a, t, sems.at[base + 2 * i], sems.at[base + 2 * i + 1], device_id=device, device_id_type=MESH
            )
            for i, (a, t) in enumerate(parts)
        ]
        return cs[:2], cs[2:]

    to_pair = halves(4, traces, assign, pair.at[1], pair_assign.at[1], (g4, b))
    wait_ready(0)
    start(to_pair[0])
    start(to_pair[1])

    def step_up():
        pl.semaphore_wait(ready.at[4], 1)
        start(to_near)

    pl.when(jnp.logical_and(up_out, far_half))(step_up)
    samples[...] = jnp.zeros(samples.shape, f32)
    for c in arrivals:
        c.wait()
    order = inverse_order(lambda r: own_assign[0, r])
    load_samples(samples, lambda r, comp: own[r, comp], order, lambda station, comp: 3 * station + comp)
    transform(samples, full, half, twiddle, left_re, left_im)
    round_ = matching[0, 0]
    bit = lax.rem(lax.div(round_, 4), 2)
    place = lax.rem(g, 4)
    to_quad = []
    for k in range(3):
        target = k + one(place <= k)
        i = exclusive_or(place, target)
        peer = g - place + target
        cs = halves(4 + 6 * i, quad.at[0], quad_assign.at[0], quad.at[i], quad_assign.at[i], (peer, b))
        to_quad.append((i, peer, cs))

    def when_ready(k):
        i, peer, _ = to_quad[k]

        @pl.when(jnp.logical_and(jnp.logical_and(ordered, settled), peer > g))
        def _():
            pl.semaphore_wait(ready.at[i], 1)

    def keep(h):
        rows = pl.ds(2 * h, 2)
        quad[0, rows] = jnp.where(bit == 1, pair[1, rows], pair[0, rows])

    wait_recv(to_pair[0])
    for r in range(4):
        quad_assign[0, 0, r] = jnp.where(bit == 1, pair_assign[1, 0, r], pair_assign[0, 0, r])
    keep(0)
    when_ready(0)
    start(to_quad[0][2][0])

    @pl.when(above)
    def _():
        for k in (1, 2):
            when_ready(k)
            start(to_quad[k][2][0])

    wait_recv(to_pair[1])
    keep(1)
    start(to_quad[0][2][1])

    @pl.when(below)
    def _():
        wait_send(to_quad[0][2][0])
        for k in (1, 2):
            when_ready(k)
            start(to_quad[k][2][0])
            start(to_quad[k][2][1])
        wait_send(to_quad[0][2][1])

    @pl.when(above)
    def _():
        for k in (1, 2):
            start(to_quad[k][2][1])

    from_quad = [
        halves(4 + 6 * i, quad.at[0], quad_assign.at[0], quad.at[i], quad_assign.at[i], (peers[i], b))
        for i in range(1, 4)
    ]

    pl.when(jnp.logical_and(up_out, near_half))(step_up)

    samples[...] = jnp.zeros(samples.shape, f32)
    slot = lax.rem(round_, 4)

    def other_row(station, comp):
        return 4 * comp + station

    def side(step, carry):
        late = one(b < 16)
        which = exclusive_or(step, one(jnp.logical_and(jnp.logical_and(first, near_half), jnp.logical_or(above, g <= late))))

        @pl.when(which == 0)
        def _():
            wait_recv(to_near)
            order = inverse_order(lambda r: near_assign[0, r])
            load_samples(samples, lambda r, comp: near[r, comp], order, other_row)

        @pl.when(which == 1)
        def _():
            for cs in from_quad:
                wait_recv(cs[0])
                wait_recv(cs[1])
            order = inverse_order(lambda r: quad_assign[slot, 0, r])
            load_samples(samples, lambda r, comp: quad[slot, r, comp], order, other_row)

        transform(samples, full, half, twiddle, right_re, right_im)
        multiply((left_re, left_im), (right_re, right_im), cross)
        result = jnp.dot(cross[...], inverse[...], preferred_element_type=f32) * SCALE
        for row in range(12):
            for comp in range(3):
                at = 16 * row + 4 * comp
                out[which, row // 3, row % 3, comp] = result[at : at + 4, :LAGS].astype(bf16)
        return carry

    lax.fori_loop(0, 2, side, 0)
    wait_send(to_pair[0])
    wait_send(to_pair[1])

    @pl.when(above)
    def _():
        wait_send(to_quad[0][2][0])
        wait_send(to_quad[0][2][1])

    for _i, _peer, cs in to_quad[1:]:
        wait_send(cs[0])
        wait_send(cs[1])
    wait_send(to_near)


def place_kernel(both, within, between, sems):
    copies = [pltpu.make_async_copy(both.at[k], out, sems.at[k]) for k, out in enumerate((within, between))]
    for c in copies:
        c.start()
    for c in copies:
        c.wait()


def shards(traces, assign, matching):
    anywhere = pl.BlockSpec(memory_space=pl.ANY)
    hbm = pl.BlockSpec(memory_space=pltpu.HBM)
    block = traces.shape
    assign = assign.reshape(1, 4)
    tables_ = [jnp.asarray(t) for t in tables()]
    result = (2, 4, 3, 3, 4, LAGS)
    both = pl.pallas_call(
        correlate_kernel,
        out_shape=jax.ShapeDtypeStruct(result, bf16),
        in_specs=[hbm] * 7,
        out_specs=pl.BlockSpec(memory_space=pltpu.VMEM),
        scratch_shapes=[
            pltpu.VMEM(block, bf16),
            pltpu.VMEM((2,) + block, bf16),
            pltpu.VMEM((4,) + block, bf16),
            pltpu.VMEM(block, bf16),
            pltpu.SMEM(matching.shape, jnp.int32),
            pltpu.SMEM((1, 4), jnp.int32),
            pltpu.SMEM((2, 1, 4), jnp.int32),
            pltpu.SMEM((4, 1, 4), jnp.int32),
            pltpu.SMEM((1, 4), jnp.int32),
            *(pltpu.VMEM(t.shape, t.dtype) for t in tables_),
            pltpu.VMEM((32, 1280), f32),
            *(pltpu.VMEM((32, NF), f32) for _ in range(4)),
            pltpu.VMEM((192, 2 * NF), bf16),
            pltpu.SemaphoreType.DMA((28,)),
            pltpu.SemaphoreType.DMA((11,)),
            pltpu.SemaphoreType.REGULAR((5,)),
        ],
        compiler_params=pltpu.CompilerParams(collective_id=0, has_side_effects=True, vmem_limit_bytes=32 << 20),
        name="correlate",
    )(*(pltpu.with_memory_space_constraint(v, pltpu.HBM) for v in (traces, assign, matching, *tables_)))
    within, between = pl.pallas_call(
        place_kernel,
        out_shape=(jax.ShapeDtypeStruct(result[1:], bf16),) * 2,
        in_specs=[anywhere],
        out_specs=(anywhere, anywhere),
        scratch_shapes=[pltpu.SemaphoreType.DMA((2,))],
        compiler_params=pltpu.CompilerParams(vmem_limit_bytes=16 << 20),
        name="place",
    )(both)
    return tuple(jnp.transpose(v, (0, 3, 1, 2, 4)) for v in (between, within))


def solution(mesh):
    placed = (P(("group", "blk"), None, None, None), P(("group", "blk")), P("blk", None))
    return jax.shard_map(
        shards,
        mesh=mesh,
        in_specs=placed,
        out_specs=(
            P(("group", "blk"), None, None, None, None),
            P(("group", "blk"), None, None, None, None),
        ),
        check_vma=False,
    )
```

```python
import functools
import math

import jax
import jax.numpy as jnp
import ml_dtypes
import numpy as np
from jax import lax
from jax.experimental import pallas as pl
from jax.experimental.pallas import tpu as pltpu
from jax.sharding import PartitionSpec as P

WIN = 2
NSAMP = 1200
PLEN = 1536
NF = 768
HALF = 200
LAGS = 401
FAST = 256
EPSILON = 1e-05
SCALE = 2.0 / (PLEN * math.sqrt(NSAMP * WIN))
ROOT3 = math.sqrt(3) / 2
MESH = pl.DeviceIdType.MESH
bf16, f32 = jnp.bfloat16, jnp.float32

FIRSTS = ((1, 256), (2, 256), (3, 128), (6, 128))
BINS = np.concatenate([first + 6 * np.arange(count) for first, count in FIRSTS])


def tables():
    n = np.arange(FAST)
    phases = 2 * np.pi * (np.outer(n, n) % FAST) / FAST
    c, s = np.cos(phases), np.sin(phases)
    full = np.block([[c, -s], [s, c]])
    half = np.concatenate([full[:, :128], full[:, 256:384]], axis=1)
    twiddle = np.zeros((64, FAST), np.float32)
    for i, (first, _) in enumerate(FIRSTS):
        phases = 2 * np.pi * n * first / PLEN
        twiddle[16 * i : 16 * i + 8] = np.cos(phases)
        twiddle[16 * i + 8 : 16 * i + 16] = np.sin(phases)
    phases = 2 * np.pi * (np.outer(BINS, np.arange(LAGS) - HALF) % PLEN) / PLEN
    inverse = np.zeros((2 * NF, 512))
    inverse[:NF, :LAGS] = np.cos(phases)
    inverse[NF:, :LAGS] = -np.sin(phases)
    low = ml_dtypes.bfloat16
    return full.astype(low), half.astype(low), twiddle, inverse.astype(low)


def flip(index, bit):
    return index + bit - 2 * bit * lax.rem(lax.div(index, bit), 2)


def inverse_order(assign):
    rows = [assign(r) for r in range(4)]
    order = []
    for s in range(4):
        found = 0
        for r in range(1, 4):
            found = jnp.where(rows[r] == s, r, found)
        order.append(found)
    return order


def load_samples(samples, block, order, row, twice=False):
    for station in range(4):
        for comp in range(3):
            both = block(order[station], comp).astype(f32)
            for w in range(2):
                at = 16 * w + row(station, comp)
                samples[at : at + 1, 0:NSAMP] = both[w : w + 1]
                if twice and comp == 2:
                    samples[at + 4 : at + 5, 0:NSAMP] = both[w : w + 1]


def transform(samples, full, half, twiddle, real, imag):
    v = [samples[:, FAST * i : FAST * i + FAST] for i in range(5)]
    energy = v[0] * v[0]
    for i in range(1, 5):
        energy = energy + v[i] * v[i]
    scale = lax.rsqrt(jnp.sum(energy, axis=-1, keepdims=True) * (1.0 / NSAMP) + EPSILON)
    even, odd = v[0] + v[2] + v[4], v[1] + v[3]
    minus, plus = v[0] - v[3], v[0] + v[3]
    parts = (
        (minus + 0.5 * (v[1] - v[2] - v[4]), -ROOT3 * (v[1] + v[2] - v[4])),
        (plus - 0.5 * (v[1] + v[2] + v[4]), -ROOT3 * (v[1] - v[2] + v[4])),
        (even - odd, None),
        (even + odd, None),
    )
    turned = []
    for i, (re, im) in enumerate(parts):
        c = jnp.tile(twiddle[16 * i : 16 * i + 8, :], (4, 1))
        s = jnp.tile(twiddle[16 * i + 8 : 16 * i + 16, :], (4, 1))
        if im is None:
            re, im = re * c, -re * s
        else:
            re, im = re * c + im * s, im * c - re * s
        turned.append(jnp.concatenate([re.astype(bf16), im.astype(bf16)], axis=1))
    column = 0
    for i, table, count in ((0, full, FAST), (2, half, 128)):
        both = jnp.concatenate(turned[i : i + 2], axis=0)
        spectra = jnp.dot(both, table[...], preferred_element_type=f32)
        for k in range(2):
            real[:, column : column + count] = spectra[32 * k : 32 * k + 32, :count] * scale
            imag[:, column : column + count] = spectra[32 * k : 32 * k + 32, count:] * scale
            column += count


def multiply(left, right, cross):
    upper = lax.broadcasted_iota(jnp.int32, (8, 256), 0) < 4
    for q in range(3):
        lanes = slice(256 * q, 256 * q + 256)

        def product(rows, at):
            re = im = None
            for w in range(2):
                left_re, left_im = (
                    [jnp.broadcast_to(part[16 * w + row : 16 * w + row + 1, lanes], (8, 256)) for row in rows]
                    for part in left
                )
                if len(rows) == 2:
                    left_re, left_im = [jnp.where(upper, *left_re)], [jnp.where(upper, *left_im)]
                right_re, right_im = (part[16 * w + at : 16 * w + at + 8, lanes] for part in right)
                a = left_re[0] * right_re + left_im[0] * right_im
                d = left_re[0] * right_im - left_im[0] * right_re
                re, im = (a, d) if re is None else (re + a, im + d)
            return re, im

        for four in range(3):
            row = 4 * four
            parts = [product((row + k,), 0) for k in range(4)] + [product((row + k, row + k + 1), 8) for k in (0, 2)]
            rows = slice(48 * four, 48 * four + 48)
            for k, column in enumerate((256 * q, NF + 256 * q)):
                cross[rows, column : column + 256] = jnp.concatenate([p[k] for p in parts], axis=0).astype(bf16)


def exclusive_or(a, b):
    a1, b1 = lax.div(a, 2), lax.div(b, 2)
    a0, b0 = a - 2 * a1, b - 2 * b1
    return 2 * (a1 + b1 - 2 * a1 * b1) + a0 + b0 - 2 * a0 * b0


def correlate_kernel(
    traces, assign, matching_hbm, full_hbm, half_hbm, twiddle_hbm, inverse_hbm,
    out,
    own, pair, quad, near, matching, own_assign, pair_assign, quad_assign, near_assign,
    full, half, twiddle, inverse, samples, left_re, left_im, right_re, right_im, cross,
    sems, local, ready,
):
    g, b = lax.axis_index("group"), lax.axis_index("blk")
    core, x, high = lax.rem(b, 2), lax.rem(lax.div(b, 2), 4), lax.rem(lax.div(b, 8), 2)
    left, right = lax.rem(b + 63, 64), lax.rem(b + 1, 64)
    last = jnp.logical_and(x == 3, core == 1)
    first = jnp.logical_and(x == 0, core == 0)
    below, above = high == 0, high == 1
    up_out = jnp.logical_and(last, below)
    up_in = jnp.logical_and(first, above)
    near_half = g < 4
    far_half = g >= 4
    plain_out = jnp.logical_not(up_out)
    plain_in = jnp.logical_not(up_in)
    opposite = lax.rem(g + 4, 8)

    g4, g1, g2 = flip(g, 4), flip(g, 1), flip(g, 2)
    g3 = flip(g1, 2)

    def copies(base, source, source_assign, target, target_assign, device):
        return [
            pltpu.make_async_remote_copy(
                a, t, sems.at[base + 2 * i], sems.at[base + 2 * i + 1], device_id=device, device_id_type=MESH
            )
            for i, (a, t) in enumerate(((source, target), (source_assign, target_assign)))
        ]

    def start(cs):
        for c in cs:
            c.start()

    def wait_recv(cs):
        for c in cs:
            c.wait_recv()

    def wait_send(cs):
        for c in cs:
            c.wait_send()

    barrier = pltpu.get_barrier_semaphore()

    def one(flag):
        return flag.astype(jnp.int32)

    def greet(device):
        pl.semaphore_signal(barrier, inc=1, device_id=device, device_id_type=MESH)

    def tell(i, device):
        pl.semaphore_signal(ready.at[i], inc=1, device_id=device, device_id_type=MESH)

    peers = (g4, g1, g2, g3)
    ordered = jnp.logical_or(below, last)
    mutual = jnp.logical_not(ordered)
    witness = jnp.logical_and(up_in, near_half)
    count = one(plain_out) + 2 * one(witness)
    source = jnp.logical_and(jnp.logical_and(above, last), near_half)
    count = count + 3 * one(jnp.logical_and(jnp.logical_and(above, last), far_half))
    settled = jnp.logical_not(source)
    for peer in peers:
        count = count + one(jnp.logical_and(settled, jnp.logical_or(mutual, peer < g)))

        @pl.when(jnp.logical_and(settled, jnp.logical_or(mutual, peer > g)))
        def _():
            greet((peer, b))

    @pl.when(source)
    def _():
        for other in range(4, 8):
            greet((other, b))

    @pl.when(plain_in)
    def _():
        greet((g, left))

    @pl.when(jnp.logical_and(up_out, near_half))
    def _():
        greet((g, right))

    @pl.when(jnp.logical_and(up_out, far_half))
    def _():
        greet((opposite, right))

    arrivals = [
        pltpu.make_async_copy(source, target, local.at[i])
        for i, (source, target) in enumerate(
            (
                (traces, own),
                (traces, pair.at[0]),
                (assign, pair_assign.at[0]),
                (assign, own_assign),
                (matching_hbm, matching),
                (full_hbm, full),
                (half_hbm, half),
                (twiddle_hbm, twiddle),
                (inverse_hbm, inverse),
            )
        )
    ]
    for c in arrivals:
        c.start()

    @pl.when(count > 0)
    def _():
        pl.semaphore_wait(barrier, count)

    to_near = copies(0, traces, assign, near, near_assign, (g, right))

    @pl.when(plain_out)
    def _():
        start(to_near)

    for i, peer in enumerate(peers):

        @pl.when(jnp.logical_and(jnp.logical_and(ordered, settled), peer < g))
        def _():
            tell(i, (peer, b))

    @pl.when(witness)
    def _():
        tell(4, (g, left))
        tell(4, (opposite, left))

    def wait_ready(i):
        @pl.when(jnp.logical_and(ordered, peers[i] > g))
        def _():
            pl.semaphore_wait(ready.at[i], 1)

    def halves(base, source, source_assign, target, target_assign, device):
        parts = (
            (source.at[pl.ds(0, 2)], target.at[pl.ds(0, 2)]),
            (source_assign, target_assign),
            (source.at[pl.ds(2, 2)], target.at[pl.ds(2, 2)]),
        )
        cs = [
            pltpu.make_async_remote_copy(
                a, t, sems.at[base + 2 * i], sems.at[base + 2 * i + 1], device_id=device, device_id_type=MESH
            )
            for i, (a, t) in enumerate(parts)
        ]
        return cs[:2], cs[2:]

    to_pair = halves(4, traces, assign, pair.at[1], pair_assign.at[1], (g4, b))
    wait_ready(0)
    start(to_pair[0])
    start(to_pair[1])

    def step_up():
        pl.semaphore_wait(ready.at[4], 1)
        start(to_near)

    pl.when(jnp.logical_and(up_out, far_half))(step_up)
    samples[...] = jnp.zeros(samples.shape, f32)
    for c in arrivals:
        c.wait()
    order = inverse_order(lambda r: own_assign[0, r])
    load_samples(samples, lambda r, comp: own[r, comp], order, lambda station, comp: 3 * station + comp)
    transform(samples, full, half, twiddle, left_re, left_im)
    round_ = matching[0, 0]
    bit = lax.rem(lax.div(round_, 4), 2)
    place = lax.rem(g, 4)
    to_quad = []
    for k in range(3):
        target = k + one(place <= k)
        i = exclusive_or(place, target)
        peer = g - place + target
        cs = halves(4 + 6 * i, quad.at[0], quad_assign.at[0], quad.at[i], quad_assign.at[i], (peer, b))
        to_quad.append((i, peer, cs))

    def when_ready(k):
        i, peer, _ = to_quad[k]

        @pl.when(jnp.logical_and(jnp.logical_and(ordered, settled), peer > g))
        def _():
            pl.semaphore_wait(ready.at[i], 1)

    def keep(h):
        rows = pl.ds(2 * h, 2)
        quad[0, rows] = jnp.where(bit == 1, pair[1, rows], pair[0, rows])

    wait_recv(to_pair[0])
    for r in range(4):
        quad_assign[0, 0, r] = jnp.where(bit == 1, pair_assign[1, 0, r], pair_assign[0, 0, r])
    keep(0)
    when_ready(0)
    start(to_quad[0][2][0])

    @pl.when(above)
    def _():
        for k in (1, 2):
            when_ready(k)
            start(to_quad[k][2][0])

    wait_recv(to_pair[1])
    keep(1)
    start(to_quad[0][2][1])

    @pl.when(below)
    def _():
        wait_send(to_quad[0][2][0])
        for k in (1, 2):
            when_ready(k)
            start(to_quad[k][2][0])
            start(to_quad[k][2][1])
        wait_send(to_quad[0][2][1])

    @pl.when(above)
    def _():
        for k in (1, 2):
            start(to_quad[k][2][1])

    from_quad = [
        halves(4 + 6 * i, quad.at[0], quad_assign.at[0], quad.at[i], quad_assign.at[i], (peers[i], b))
        for i in range(1, 4)
    ]

    pl.when(jnp.logical_and(up_out, near_half))(step_up)

    samples[...] = jnp.zeros(samples.shape, f32)
    slot = lax.rem(round_, 4)

    def other_row(station, comp):
        return 4 * comp + station

    def side(step, carry):
        late = one(b < 16)
        which = exclusive_or(step, one(jnp.logical_and(jnp.logical_and(first, near_half), jnp.logical_or(above, g <= late))))

        @pl.when(which == 0)
        def _():
            wait_recv(to_near)
            order = inverse_order(lambda r: near_assign[0, r])
            load_samples(samples, lambda r, comp: near[r, comp], order, other_row, True)

        @pl.when(which == 1)
        def _():
            for cs in from_quad:
                wait_recv(cs[0])
                wait_recv(cs[1])
            order = inverse_order(lambda r: quad_assign[slot, 0, r])
            load_samples(samples, lambda r, comp: quad[slot, r, comp], order, other_row, True)

        transform(samples, full, half, twiddle, right_re, right_im)
        multiply((left_re, left_im), (right_re, right_im), cross)
        result = jnp.dot(cross[...], inverse[...], preferred_element_type=f32) * SCALE
        for row in range(12):
            for comp in range(3):
                at = 48 * (row // 4) + (32 + 4 * (row % 4) if comp == 2 else 8 * (row % 4) + 4 * comp)
                out[which, row // 3, row % 3, comp] = result[at : at + 4, :LAGS].astype(bf16)
        return carry

    lax.fori_loop(0, 2, side, 0)
    wait_send(to_pair[0])
    wait_send(to_pair[1])

    @pl.when(above)
    def _():
        wait_send(to_quad[0][2][0])
        wait_send(to_quad[0][2][1])

    for _i, _peer, cs in to_quad[1:]:
        wait_send(cs[0])
        wait_send(cs[1])
    wait_send(to_near)


def place_kernel(both, within, between, sems):
    copies = [pltpu.make_async_copy(both.at[k], out, sems.at[k]) for k, out in enumerate((within, between))]
    for c in copies:
        c.start()
    for c in copies:
        c.wait()


def shards(traces, assign, matching):
    anywhere = pl.BlockSpec(memory_space=pl.ANY)
    hbm = pl.BlockSpec(memory_space=pltpu.HBM)
    block = traces.shape
    assign = assign.reshape(1, 4)
    tables_ = [jnp.asarray(t) for t in tables()]
    result = (2, 4, 3, 3, 4, LAGS)
    both = pl.pallas_call(
        correlate_kernel,
        out_shape=jax.ShapeDtypeStruct(result, bf16),
        in_specs=[hbm] * 7,
        out_specs=pl.BlockSpec(memory_space=pltpu.VMEM),
        scratch_shapes=[
            pltpu.VMEM(block, bf16),
            pltpu.VMEM((2,) + block, bf16),
            pltpu.VMEM((4,) + block, bf16),
            pltpu.VMEM(block, bf16),
            pltpu.SMEM(matching.shape, jnp.int32),
            pltpu.SMEM((1, 4), jnp.int32),
            pltpu.SMEM((2, 1, 4), jnp.int32),
            pltpu.SMEM((4, 1, 4), jnp.int32),
            pltpu.SMEM((1, 4), jnp.int32),
            *(pltpu.VMEM(t.shape, t.dtype) for t in tables_),
            pltpu.VMEM((32, 1280), f32),
            *(pltpu.VMEM((32, NF), f32) for _ in range(4)),
            pltpu.VMEM((144, 2 * NF), bf16),
            pltpu.SemaphoreType.DMA((28,)),
            pltpu.SemaphoreType.DMA((11,)),
            pltpu.SemaphoreType.REGULAR((5,)),
        ],
        compiler_params=pltpu.CompilerParams(collective_id=0, has_side_effects=True, vmem_limit_bytes=32 << 20),
        name="correlate",
    )(*(pltpu.with_memory_space_constraint(v, pltpu.HBM) for v in (traces, assign, matching, *tables_)))
    within, between = pl.pallas_call(
        place_kernel,
        out_shape=(jax.ShapeDtypeStruct(result[1:], bf16),) * 2,
        in_specs=[anywhere],
        out_specs=(anywhere, anywhere),
        scratch_shapes=[pltpu.SemaphoreType.DMA((2,))],
        compiler_params=pltpu.CompilerParams(vmem_limit_bytes=16 << 20),
        name="place",
    )(both)
    return tuple(jnp.transpose(v, (0, 3, 1, 2, 4)) for v in (between, within))


def solution(mesh):
    placed = (P(("group", "blk"), None, None, None), P(("group", "blk")), P("blk", None))
    return jax.shard_map(
        shards,
        mesh=mesh,
        in_specs=placed,
        out_specs=(
            P(("group", "blk"), None, None, None, None),
            P(("group", "blk"), None, None, None, None),
        ),
        check_vma=False,
    )
```

```python
import functools
import math

import jax
import jax.numpy as jnp
import ml_dtypes
import numpy as np
from jax import lax
from jax.experimental import pallas as pl
from jax.experimental.pallas import tpu as pltpu
from jax.sharding import PartitionSpec as P

WIN = 2
NSAMP = 1200
PLEN = 1536
NF = 768
HALF = 200
LAGS = 401
FAST = 256
PIECES = 4
HEAD = 4
STEP = 2 * PIECES + 2
EPSILON = 1e-05
SCALE = 2.0 / (PLEN * math.sqrt(NSAMP * WIN))
ROOT3 = math.sqrt(3) / 2
MESH = pl.DeviceIdType.MESH
bf16, f32 = jnp.bfloat16, jnp.float32

FIRSTS = ((1, 256), (2, 256), (3, 128), (6, 128))
BINS = np.concatenate([first + 6 * np.arange(count) for first, count in FIRSTS])


def tables():
    n = np.arange(FAST)
    phases = 2 * np.pi * (np.outer(n, n) % FAST) / FAST
    c, s = np.cos(phases), np.sin(phases)
    full = np.block([[c, -s], [s, c]])
    half = np.concatenate([full[:, :128], full[:, 256:384]], axis=1)
    twiddle = np.zeros((64, FAST), np.float32)
    for i, (first, _) in enumerate(FIRSTS):
        phases = 2 * np.pi * n * first / PLEN
        twiddle[16 * i : 16 * i + 8] = np.cos(phases)
        twiddle[16 * i + 8 : 16 * i + 16] = np.sin(phases)
    phases = 2 * np.pi * (np.outer(BINS, np.arange(LAGS) - HALF) % PLEN) / PLEN
    inverse = np.zeros((2 * NF, 512))
    inverse[:NF, :LAGS] = np.cos(phases)
    inverse[NF:, :LAGS] = -np.sin(phases)
    low = ml_dtypes.bfloat16
    return full.astype(low), half.astype(low), twiddle, inverse.astype(low)


def flip(index, bit):
    return index + bit - 2 * bit * lax.rem(lax.div(index, bit), 2)


def inverse_order(assign):
    rows = [assign(r) for r in range(4)]
    order = []
    for s in range(4):
        found = 0
        for r in range(1, 4):
            found = jnp.where(rows[r] == s, r, found)
        order.append(found)
    return order


def load_samples(samples, block, order, row, twice=False):
    for station in range(4):
        for comp in range(3):
            both = block(order[station], comp).astype(f32)
            for w in range(2):
                at = 16 * w + row(station, comp)
                samples[at : at + 1, 0:NSAMP] = both[w : w + 1]
                if twice and comp == 2:
                    samples[at + 4 : at + 5, 0:NSAMP] = both[w : w + 1]


def transform(samples, full, half, twiddle, real, imag):
    v = [samples[:, FAST * i : FAST * i + FAST] for i in range(5)]
    energy = v[0] * v[0]
    for i in range(1, 5):
        energy = energy + v[i] * v[i]
    scale = lax.rsqrt(jnp.sum(energy, axis=-1, keepdims=True) * (1.0 / NSAMP) + EPSILON)
    even, odd = v[0] + v[2] + v[4], v[1] + v[3]
    minus, plus = v[0] - v[3], v[0] + v[3]
    parts = (
        (minus + 0.5 * (v[1] - v[2] - v[4]), -ROOT3 * (v[1] + v[2] - v[4])),
        (plus - 0.5 * (v[1] + v[2] + v[4]), -ROOT3 * (v[1] - v[2] + v[4])),
        (even - odd, None),
        (even + odd, None),
    )
    turned = []
    for i, (re, im) in enumerate(parts):
        c = jnp.tile(twiddle[16 * i : 16 * i + 8, :], (4, 1))
        s = jnp.tile(twiddle[16 * i + 8 : 16 * i + 16, :], (4, 1))
        if im is None:
            re, im = re * c, -re * s
        else:
            re, im = re * c + im * s, im * c - re * s
        turned.append(jnp.concatenate([re.astype(bf16), im.astype(bf16)], axis=1))
    column = 0
    for i, table, count in ((0, full, FAST), (2, half, 128)):
        both = jnp.concatenate(turned[i : i + 2], axis=0)
        spectra = jnp.dot(both, table[...], preferred_element_type=f32)
        for k in range(2):
            real[:, column : column + count] = spectra[32 * k : 32 * k + 32, :count] * scale
            imag[:, column : column + count] = spectra[32 * k : 32 * k + 32, count:] * scale
            column += count


def multiply(left, right, cross):
    upper = lax.broadcasted_iota(jnp.int32, (8, 256), 0) < 4
    for q in range(3):
        lanes = slice(256 * q, 256 * q + 256)

        def product(rows, at):
            re = im = None
            for w in range(2):
                left_re, left_im = (
                    [jnp.broadcast_to(part[16 * w + row : 16 * w + row + 1, lanes], (8, 256)) for row in rows]
                    for part in left
                )
                if len(rows) == 2:
                    left_re, left_im = [jnp.where(upper, *left_re)], [jnp.where(upper, *left_im)]
                right_re, right_im = (part[16 * w + at : 16 * w + at + 8, lanes] for part in right)
                a = left_re[0] * right_re + left_im[0] * right_im
                d = left_re[0] * right_im - left_im[0] * right_re
                re, im = (a, d) if re is None else (re + a, im + d)
            return re, im

        for four in range(3):
            row = 4 * four
            parts = [product((row + k,), 0) for k in range(4)] + [product((row + k, row + k + 1), 8) for k in (0, 2)]
            rows = slice(48 * four, 48 * four + 48)
            for k, column in enumerate((256 * q, NF + 256 * q)):
                cross[rows, column : column + 256] = jnp.concatenate([p[k] for p in parts], axis=0).astype(bf16)


def exclusive_or(a, b):
    a1, b1 = lax.div(a, 2), lax.div(b, 2)
    a0, b0 = a - 2 * a1, b - 2 * b1
    return 2 * (a1 + b1 - 2 * a1 * b1) + a0 + b0 - 2 * a0 * b0


def correlate_kernel(
    traces, assign, matching_hbm, full_hbm, half_hbm, twiddle_hbm, inverse_hbm,
    out,
    own, pair, quad, near, matching, own_assign, pair_assign, quad_assign, near_assign,
    full, half, twiddle, inverse, samples, left_re, left_im, right_re, right_im, cross,
    sems, local, ready,
):
    g, b = lax.axis_index("group"), lax.axis_index("blk")
    core, x, high = lax.rem(b, 2), lax.rem(lax.div(b, 2), 4), lax.rem(lax.div(b, 8), 2)
    left, right = lax.rem(b + 63, 64), lax.rem(b + 1, 64)
    last = jnp.logical_and(x == 3, core == 1)
    first = jnp.logical_and(x == 0, core == 0)
    below, above = high == 0, high == 1
    up_out = jnp.logical_and(last, below)
    up_in = jnp.logical_and(first, above)
    near_half = g < 4
    far_half = g >= 4
    plain_out = jnp.logical_not(up_out)
    plain_in = jnp.logical_not(up_in)
    opposite = lax.rem(g + 4, 8)

    g4, g1, g2 = flip(g, 4), flip(g, 1), flip(g, 2)
    g3 = flip(g1, 2)

    def copies(base, source, source_assign, target, target_assign, device):
        return [
            pltpu.make_async_remote_copy(
                a, t, sems.at[base + 2 * i], sems.at[base + 2 * i + 1], device_id=device, device_id_type=MESH
            )
            for i, (a, t) in enumerate(((source, target), (source_assign, target_assign)))
        ]

    def start(cs):
        for c in cs:
            c.start()

    def wait_recv(cs):
        for c in cs:
            c.wait_recv()

    def wait_send(cs):
        for c in cs:
            c.wait_send()

    barrier = pltpu.get_barrier_semaphore()

    def one(flag):
        return flag.astype(jnp.int32)

    def greet(device):
        pl.semaphore_signal(barrier, inc=1, device_id=device, device_id_type=MESH)

    def tell(i, device):
        pl.semaphore_signal(ready.at[i], inc=1, device_id=device, device_id_type=MESH)

    peers = (g4, g1, g2, g3)
    ordered = jnp.logical_or(below, last)
    mutual = jnp.logical_not(ordered)
    witness = jnp.logical_and(up_in, near_half)
    count = one(plain_out) + 2 * one(witness)
    source = jnp.logical_and(jnp.logical_and(above, last), near_half)
    count = count + 3 * one(jnp.logical_and(jnp.logical_and(above, last), far_half))
    settled = jnp.logical_not(source)
    for peer in peers:
        count = count + one(jnp.logical_and(settled, jnp.logical_or(mutual, peer < g)))

        @pl.when(jnp.logical_and(settled, jnp.logical_or(mutual, peer > g)))
        def _():
            greet((peer, b))

    @pl.when(source)
    def _():
        for other in range(4, 8):
            greet((other, b))

    @pl.when(plain_in)
    def _():
        greet((g, left))

    @pl.when(jnp.logical_and(up_out, near_half))
    def _():
        greet((g, right))

    @pl.when(jnp.logical_and(up_out, far_half))
    def _():
        greet((opposite, right))

    arrivals = [
        pltpu.make_async_copy(source, target, local.at[i])
        for i, (source, target) in enumerate(
            (
                (traces, own),
                (traces, pair.at[0]),
                (assign, pair_assign.at[0]),
                (assign, own_assign),
                (matching_hbm, matching),
                (full_hbm, full),
                (half_hbm, half),
                (twiddle_hbm, twiddle),
                (inverse_hbm, inverse),
            )
        )
    ]
    for c in arrivals:
        c.start()

    @pl.when(count > 0)
    def _():
        pl.semaphore_wait(barrier, count)

    to_near = copies(0, traces, assign, near, near_assign, (g, right))

    @pl.when(plain_out)
    def _():
        start(to_near)

    for i, peer in enumerate(peers):

        @pl.when(jnp.logical_and(jnp.logical_and(ordered, settled), peer < g))
        def _():
            tell(i, (peer, b))

    @pl.when(witness)
    def _():
        tell(4, (g, left))
        tell(4, (opposite, left))

    def wait_ready(i):
        @pl.when(jnp.logical_and(ordered, peers[i] > g))
        def _():
            pl.semaphore_wait(ready.at[i], 1)

    def pieces(base, source, source_assign, target, target_assign, device):
        rows = source.shape[0] // PIECES
        parts = [(source.at[pl.ds(rows * h, rows)], target.at[pl.ds(rows * h, rows)]) for h in range(PIECES)]
        cs = [
            pltpu.make_async_remote_copy(
                a, t, sems.at[base + 2 * i], sems.at[base + 2 * i + 1], device_id=device, device_id_type=MESH
            )
            for i, (a, t) in enumerate([*parts, (source_assign, target_assign)])
        ]
        return [[cs[0], cs[-1]]] + [[c] for c in cs[1:-1]]

    to_pair = pieces(4, traces, assign, pair.at[1], pair_assign.at[1], (g4, b))
    wait_ready(0)
    for cs in to_pair:
        start(cs)

    def step_up():
        pl.semaphore_wait(ready.at[4], 1)
        start(to_near)

    pl.when(jnp.logical_and(up_out, far_half))(step_up)
    samples[...] = jnp.zeros(samples.shape, f32)
    for c in arrivals:
        c.wait()
    order = inverse_order(lambda r: own_assign[0, r])
    load_samples(samples, lambda r, comp: own[r, comp], order, lambda station, comp: 3 * station + comp)
    transform(samples, full, half, twiddle, left_re, left_im)
    round_ = matching[0, 0]
    bit = lax.rem(lax.div(round_, 4), 2)
    place = lax.rem(g, 4)
    to_quad = []
    for k in range(3):
        target = k + one(place <= k)
        i = exclusive_or(place, target)
        peer = g - place + target
        cs = pieces(4 + STEP * i, quad.at[0], quad_assign.at[0], quad.at[i], quad_assign.at[i], (peer, b))
        to_quad.append((i, peer, cs))

    def when_ready(k):
        i, peer, _ = to_quad[k]

        @pl.when(jnp.logical_and(jnp.logical_and(ordered, settled), peer > g))
        def _():
            pl.semaphore_wait(ready.at[i], 1)

    def keep(h):
        rows = pl.ds(h * (4 // PIECES), 4 // PIECES)
        quad[0, rows] = jnp.where(bit == 1, pair[1, rows], pair[0, rows])

    for h in range(PIECES):
        wait_recv(to_pair[h])
        if h == 0:
            for r in range(4):
                quad_assign[0, 0, r] = jnp.where(bit == 1, pair_assign[1, 0, r], pair_assign[0, 0, r])
            when_ready(0)
        keep(h)
        start(to_quad[0][2][h])

        @pl.when(above)
        def _():
            for k in (1, 2):
                if h == 0:
                    when_ready(k)
                start(to_quad[k][2][h])

    @pl.when(below)
    def _():
        for h in range(PIECES // HEAD):
            wait_send(to_quad[0][2][h])
        for k in (1, 2):
            when_ready(k)
            for cs in to_quad[k][2]:
                start(cs)
        for h in range(PIECES // HEAD, PIECES):
            wait_send(to_quad[0][2][h])

    from_quad = [
        pieces(4 + STEP * i, quad.at[0], quad_assign.at[0], quad.at[i], quad_assign.at[i], (peers[i], b))
        for i in range(1, 4)
    ]

    pl.when(jnp.logical_and(up_out, near_half))(step_up)

    samples[...] = jnp.zeros(samples.shape, f32)
    slot = lax.rem(round_, 4)

    def other_row(station, comp):
        return 4 * comp + station

    def side(step, carry):
        late = one(b < 16)
        which = exclusive_or(step, one(jnp.logical_and(jnp.logical_and(first, near_half), jnp.logical_or(above, g <= late))))

        @pl.when(which == 0)
        def _():
            wait_recv(to_near)
            order = inverse_order(lambda r: near_assign[0, r])
            load_samples(samples, lambda r, comp: near[r, comp], order, other_row, True)

        @pl.when(which == 1)
        def _():
            for cs in from_quad:
                for piece in cs:
                    wait_recv(piece)
            order = inverse_order(lambda r: quad_assign[slot, 0, r])
            load_samples(samples, lambda r, comp: quad[slot, r, comp], order, other_row, True)

        transform(samples, full, half, twiddle, right_re, right_im)
        multiply((left_re, left_im), (right_re, right_im), cross)
        result = jnp.dot(cross[...], inverse[...], preferred_element_type=f32) * SCALE
        for row in range(12):
            for comp in range(3):
                at = 48 * (row // 4) + (32 + 4 * (row % 4) if comp == 2 else 8 * (row % 4) + 4 * comp)
                out[which, row // 3, row % 3, comp] = result[at : at + 4, :LAGS].astype(bf16)
        return carry

    lax.fori_loop(0, 2, side, 0)
    for cs in to_pair:
        wait_send(cs)

    @pl.when(above)
    def _():
        for cs in to_quad[0][2]:
            wait_send(cs)

    for _i, _peer, sent in to_quad[1:]:
        for cs in sent:
            wait_send(cs)
    wait_send(to_near)


def place_kernel(both, within, between, sems):
    copies = [pltpu.make_async_copy(both.at[k], out, sems.at[k]) for k, out in enumerate((within, between))]
    for c in copies:
        c.start()
    for c in copies:
        c.wait()


def shards(traces, assign, matching):
    anywhere = pl.BlockSpec(memory_space=pl.ANY)
    hbm = pl.BlockSpec(memory_space=pltpu.HBM)
    block = traces.shape
    assign = assign.reshape(1, 4)
    tables_ = [jnp.asarray(t) for t in tables()]
    result = (2, 4, 3, 3, 4, LAGS)
    both = pl.pallas_call(
        correlate_kernel,
        out_shape=jax.ShapeDtypeStruct(result, bf16),
        in_specs=[hbm] * 7,
        out_specs=pl.BlockSpec(memory_space=pltpu.VMEM),
        scratch_shapes=[
            pltpu.VMEM(block, bf16),
            pltpu.VMEM((2,) + block, bf16),
            pltpu.VMEM((4,) + block, bf16),
            pltpu.VMEM(block, bf16),
            pltpu.SMEM(matching.shape, jnp.int32),
            pltpu.SMEM((1, 4), jnp.int32),
            pltpu.SMEM((2, 1, 4), jnp.int32),
            pltpu.SMEM((4, 1, 4), jnp.int32),
            pltpu.SMEM((1, 4), jnp.int32),
            *(pltpu.VMEM(t.shape, t.dtype) for t in tables_),
            pltpu.VMEM((32, 1280), f32),
            *(pltpu.VMEM((32, NF), f32) for _ in range(4)),
            pltpu.VMEM((144, 2 * NF), bf16),
            pltpu.SemaphoreType.DMA((4 + 4 * STEP,)),
            pltpu.SemaphoreType.DMA((11,)),
            pltpu.SemaphoreType.REGULAR((5,)),
        ],
        compiler_params=pltpu.CompilerParams(collective_id=0, has_side_effects=True, vmem_limit_bytes=32 << 20),
        name="correlate",
    )(*(pltpu.with_memory_space_constraint(v, pltpu.HBM) for v in (traces, assign, matching, *tables_)))
    within, between = pl.pallas_call(
        place_kernel,
        out_shape=(jax.ShapeDtypeStruct(result[1:], bf16),) * 2,
        in_specs=[anywhere],
        out_specs=(anywhere, anywhere),
        scratch_shapes=[pltpu.SemaphoreType.DMA((2,))],
        compiler_params=pltpu.CompilerParams(vmem_limit_bytes=16 << 20),
        name="place",
    )(both)
    return tuple(jnp.transpose(v, (0, 3, 1, 2, 4)) for v in (between, within))


def solution(mesh):
    placed = (P(("group", "blk"), None, None, None), P(("group", "blk")), P("blk", None))
    return jax.shard_map(
        shards,
        mesh=mesh,
        in_specs=placed,
        out_specs=(
            P(("group", "blk"), None, None, None, None),
            P(("group", "blk"), None, None, None, None),
        ),
        check_vma=False,
    )
```

```python
import functools
import math

import jax
import jax.numpy as jnp
import ml_dtypes
import numpy as np
from jax import lax
from jax.experimental import pallas as pl
from jax.experimental.pallas import tpu as pltpu
from jax.sharding import PartitionSpec as P

WIN = 2
NSAMP = 1200
PLEN = 1536
NF = 768
HALF = 200
LAGS = 401
FAST = 256
PIECES = 4
HEAD = 4
STEP = 2 * PIECES + 2
EPSILON = 1e-05
SCALE = 2.0 / (PLEN * math.sqrt(NSAMP * WIN))
ROOT3 = math.sqrt(3) / 2
MESH = pl.DeviceIdType.MESH
bf16, f32 = jnp.bfloat16, jnp.float32

FIRSTS = ((1, 256), (2, 256), (3, 128), (6, 128))
BINS = np.concatenate([first + 6 * np.arange(count) for first, count in FIRSTS])


def tables():
    n = np.arange(FAST)
    phases = 2 * np.pi * (np.outer(n, n) % FAST) / FAST
    c, s = np.cos(phases), np.sin(phases)
    full = np.block([[c, -s], [s, c]])
    half = np.concatenate([full[:, :128], full[:, 256:384]], axis=1)
    twiddle = np.zeros((64, FAST), np.float32)
    for i, (first, _) in enumerate(FIRSTS):
        phases = 2 * np.pi * n * first / PLEN
        twiddle[16 * i : 16 * i + 8] = np.cos(phases)
        twiddle[16 * i + 8 : 16 * i + 16] = np.sin(phases)
    phases = 2 * np.pi * (np.outer(BINS, np.arange(LAGS) - HALF) % PLEN) / PLEN
    inverse = np.zeros((2 * NF, 512))
    inverse[:NF, :LAGS] = np.cos(phases)
    inverse[NF:, :LAGS] = -np.sin(phases)
    low = ml_dtypes.bfloat16
    return full.astype(low), half.astype(low), twiddle, inverse.astype(low)


def flip(index, bit):
    return index + bit - 2 * bit * lax.rem(lax.div(index, bit), 2)


def inverse_order(assign):
    rows = [assign(r) for r in range(4)]
    order = []
    for s in range(4):
        found = 0
        for r in range(1, 4):
            found = jnp.where(rows[r] == s, r, found)
        order.append(found)
    return order


def load_samples(samples, block, order, row, twice=False):
    for station in range(4):
        for comp in range(3):
            both = block(order[station], comp).astype(f32)
            for w in range(2):
                at = 16 * w + row(station, comp)
                samples[at : at + 1, 0:NSAMP] = both[w : w + 1]
                if twice and comp == 2:
                    samples[at + 4 : at + 5, 0:NSAMP] = both[w : w + 1]


def transform(samples, full, half, twiddle, real, imag):
    v = [samples[:, FAST * i : FAST * i + FAST] for i in range(5)]
    energy = v[0] * v[0]
    for i in range(1, 5):
        energy = energy + v[i] * v[i]
    scale = lax.rsqrt(jnp.sum(energy, axis=-1, keepdims=True) * (1.0 / NSAMP) + EPSILON)
    even, odd = v[0] + v[2] + v[4], v[1] + v[3]
    minus, plus = v[0] - v[3], v[0] + v[3]
    parts = (
        (minus + 0.5 * (v[1] - v[2] - v[4]), -ROOT3 * (v[1] + v[2] - v[4])),
        (plus - 0.5 * (v[1] + v[2] + v[4]), -ROOT3 * (v[1] - v[2] + v[4])),
        (even - odd, None),
        (even + odd, None),
    )
    turned = []
    for i, (re, im) in enumerate(parts):
        c = jnp.tile(twiddle[16 * i : 16 * i + 8, :], (4, 1))
        s = jnp.tile(twiddle[16 * i + 8 : 16 * i + 16, :], (4, 1))
        if im is None:
            re, im = re * c, -re * s
        else:
            re, im = re * c + im * s, im * c - re * s
        turned.append(jnp.concatenate([re.astype(bf16), im.astype(bf16)], axis=1))
    column = 0
    for i, table, count in ((0, full, FAST), (2, half, 128)):
        both = jnp.concatenate(turned[i : i + 2], axis=0)
        spectra = jnp.dot(both, table[...], preferred_element_type=f32)
        for k in range(2):
            real[:, column : column + count] = spectra[32 * k : 32 * k + 32, :count] * scale
            imag[:, column : column + count] = spectra[32 * k : 32 * k + 32, count:] * scale
            column += count


def multiply(left, right, cross):
    upper = lax.broadcasted_iota(jnp.int32, (8, 256), 0) < 4
    for q in range(3):
        lanes = slice(256 * q, 256 * q + 256)

        def product(rows, at):
            re = im = None
            for w in range(2):
                left_re, left_im = (
                    [jnp.broadcast_to(part[16 * w + row : 16 * w + row + 1, lanes], (8, 256)) for row in rows]
                    for part in left
                )
                if len(rows) == 2:
                    left_re, left_im = [jnp.where(upper, *left_re)], [jnp.where(upper, *left_im)]
                right_re, right_im = (part[16 * w + at : 16 * w + at + 8, lanes] for part in right)
                a = left_re[0] * right_re + left_im[0] * right_im
                d = left_re[0] * right_im - left_im[0] * right_re
                re, im = (a, d) if re is None else (re + a, im + d)
            return re, im

        for four in range(3):
            row = 4 * four
            parts = [product((row + k,), 0) for k in range(4)] + [product((row + k, row + k + 1), 8) for k in (0, 2)]
            rows = slice(48 * four, 48 * four + 48)
            for k, column in enumerate((256 * q, NF + 256 * q)):
                cross[rows, column : column + 256] = jnp.concatenate([p[k] for p in parts], axis=0).astype(bf16)


def exclusive_or(a, b):
    a1, b1 = lax.div(a, 2), lax.div(b, 2)
    a0, b0 = a - 2 * a1, b - 2 * b1
    return 2 * (a1 + b1 - 2 * a1 * b1) + a0 + b0 - 2 * a0 * b0


def correlate_kernel(
    traces, assign, matching_hbm, full_hbm, half_hbm, twiddle_hbm, inverse_hbm,
    out,
    own, pair, quad, near, matching, own_assign, pair_assign, quad_assign, near_assign,
    full, half, twiddle, inverse, samples, left_re, left_im, right_re, right_im, cross,
    sems, local, ready,
):
    g, b = lax.axis_index("group"), lax.axis_index("blk")
    core, x, high = lax.rem(b, 2), lax.rem(lax.div(b, 2), 4), lax.rem(lax.div(b, 8), 2)
    left, right = lax.rem(b + 63, 64), lax.rem(b + 1, 64)
    last = jnp.logical_and(x == 3, core == 1)
    first = jnp.logical_and(x == 0, core == 0)
    below, above = high == 0, high == 1
    up_out = jnp.logical_and(last, below)
    up_in = jnp.logical_and(first, above)
    near_half = g < 4
    far_half = g >= 4
    plain_out = jnp.logical_not(up_out)
    plain_in = jnp.logical_not(up_in)
    opposite = lax.rem(g + 4, 8)

    g4, g1, g2 = flip(g, 4), flip(g, 1), flip(g, 2)
    g3 = flip(g1, 2)

    def copies(base, source, source_assign, target, target_assign, device):
        return [
            pltpu.make_async_remote_copy(
                a, t, sems.at[base + 2 * i], sems.at[base + 2 * i + 1], device_id=device, device_id_type=MESH
            )
            for i, (a, t) in enumerate(((source, target), (source_assign, target_assign)))
        ]

    def start(cs):
        for c in cs:
            c.start()

    def wait_recv(cs):
        for c in cs:
            c.wait_recv()

    def wait_send(cs):
        for c in cs:
            c.wait_send()

    barrier = pltpu.get_barrier_semaphore()

    def one(flag):
        return flag.astype(jnp.int32)

    def greet(device):
        pl.semaphore_signal(barrier, inc=1, device_id=device, device_id_type=MESH)

    def tell(i, device):
        pl.semaphore_signal(ready.at[i], inc=1, device_id=device, device_id_type=MESH)

    peers = (g4, g1, g2, g3)
    ordered = jnp.logical_or(below, last)
    mutual = jnp.logical_not(ordered)
    witness = jnp.logical_and(up_in, near_half)
    count = one(plain_out) + 2 * one(witness)
    source = jnp.logical_and(jnp.logical_and(above, last), near_half)
    count = count + 3 * one(jnp.logical_and(jnp.logical_and(above, last), far_half))
    settled = jnp.logical_not(source)
    for peer in peers:
        count = count + one(jnp.logical_and(settled, jnp.logical_or(mutual, peer < g)))

        @pl.when(jnp.logical_and(settled, jnp.logical_or(mutual, peer > g)))
        def _():
            greet((peer, b))

    @pl.when(source)
    def _():
        for other in range(4, 8):
            greet((other, b))

    @pl.when(plain_in)
    def _():
        greet((g, left))

    @pl.when(jnp.logical_and(up_out, near_half))
    def _():
        greet((g, right))

    @pl.when(jnp.logical_and(up_out, far_half))
    def _():
        greet((opposite, right))

    arrivals = [
        pltpu.make_async_copy(source, target, local.at[i])
        for i, (source, target) in enumerate(
            (
                (traces, own),
                (traces, pair.at[0]),
                (assign, pair_assign.at[0]),
                (assign, own_assign),
                (matching_hbm, matching),
                (full_hbm, full),
                (half_hbm, half),
                (twiddle_hbm, twiddle),
                (inverse_hbm, inverse),
            )
        )
    ]
    for c in arrivals:
        c.start()

    @pl.when(count > 0)
    def _():
        pl.semaphore_wait(barrier, count)

    to_near = copies(0, traces, assign, near, near_assign, (g, right))

    for i, peer in enumerate(peers):

        @pl.when(jnp.logical_and(jnp.logical_and(ordered, settled), peer < g))
        def _():
            tell(i, (peer, b))

    @pl.when(witness)
    def _():
        tell(4, (g, left))
        tell(4, (opposite, left))

    @pl.when(plain_out)
    def _():
        start(to_near)

    def wait_ready(i):
        @pl.when(jnp.logical_and(ordered, peers[i] > g))
        def _():
            pl.semaphore_wait(ready.at[i], 1)

    def pieces(base, source, source_assign, target, target_assign, device):
        rows = source.shape[0] // PIECES
        parts = [(source.at[pl.ds(rows * h, rows)], target.at[pl.ds(rows * h, rows)]) for h in range(PIECES)]
        cs = [
            pltpu.make_async_remote_copy(
                a, t, sems.at[base + 2 * i], sems.at[base + 2 * i + 1], device_id=device, device_id_type=MESH
            )
            for i, (a, t) in enumerate([*parts, (source_assign, target_assign)])
        ]
        return [[cs[0], cs[-1]]] + [[c] for c in cs[1:-1]]

    to_pair = pieces(4, traces, assign, pair.at[1], pair_assign.at[1], (g4, b))
    wait_ready(0)
    for cs in to_pair:
        start(cs)

    def step_up():
        pl.semaphore_wait(ready.at[4], 1)
        start(to_near)

    pl.when(jnp.logical_and(up_out, far_half))(step_up)
    samples[...] = jnp.zeros(samples.shape, f32)
    for c in arrivals:
        c.wait()
    order = inverse_order(lambda r: own_assign[0, r])
    load_samples(samples, lambda r, comp: own[r, comp], order, lambda station, comp: 3 * station + comp)
    transform(samples, full, half, twiddle, left_re, left_im)
    round_ = matching[0, 0]
    bit = lax.rem(lax.div(round_, 4), 2)
    place = lax.rem(g, 4)
    to_quad = []
    for k in range(3):
        target = k + one(place <= k)
        i = exclusive_or(place, target)
        peer = g - place + target
        cs = pieces(4 + STEP * i, quad.at[0], quad_assign.at[0], quad.at[i], quad_assign.at[i], (peer, b))
        to_quad.append((i, peer, cs))

    def when_ready(k):
        i, peer, _ = to_quad[k]

        @pl.when(jnp.logical_and(jnp.logical_and(ordered, settled), peer > g))
        def _():
            pl.semaphore_wait(ready.at[i], 1)

    def keep(h):
        rows = pl.ds(h * (4 // PIECES), 4 // PIECES)
        quad[0, rows] = jnp.where(bit == 1, pair[1, rows], pair[0, rows])

    for h in range(PIECES):
        wait_recv(to_pair[h])
        if h == 0:
            for r in range(4):
                quad_assign[0, 0, r] = jnp.where(bit == 1, pair_assign[1, 0, r], pair_assign[0, 0, r])
            when_ready(0)
        keep(h)
        start(to_quad[0][2][h])

        @pl.when(above)
        def _():
            for k in (1, 2):
                if h == 0:
                    when_ready(k)
                start(to_quad[k][2][h])

    @pl.when(below)
    def _():
        for h in range(PIECES // HEAD):
            wait_send(to_quad[0][2][h])
        for k in (1, 2):
            when_ready(k)
            for cs in to_quad[k][2]:
                start(cs)
        for h in range(PIECES // HEAD, PIECES):
            wait_send(to_quad[0][2][h])

    from_quad = [
        pieces(4 + STEP * i, quad.at[0], quad_assign.at[0], quad.at[i], quad_assign.at[i], (peers[i], b))
        for i in range(1, 4)
    ]

    pl.when(jnp.logical_and(up_out, near_half))(step_up)

    samples[...] = jnp.zeros(samples.shape, f32)
    slot = lax.rem(round_, 4)

    def other_row(station, comp):
        return 4 * comp + station

    def side(step, carry):
        late = one(b < 16)
        which = exclusive_or(step, one(jnp.logical_and(jnp.logical_and(first, near_half), jnp.logical_or(above, g <= late))))

        @pl.when(which == 0)
        def _():
            wait_recv(to_near)
            order = inverse_order(lambda r: near_assign[0, r])
            load_samples(samples, lambda r, comp: near[r, comp], order, other_row, True)

        @pl.when(which == 1)
        def _():
            for cs in from_quad:
                for piece in cs:
                    wait_recv(piece)
            order = inverse_order(lambda r: quad_assign[slot, 0, r])
            load_samples(samples, lambda r, comp: quad[slot, r, comp], order, other_row, True)

        transform(samples, full, half, twiddle, right_re, right_im)
        multiply((left_re, left_im), (right_re, right_im), cross)
        result = jnp.dot(cross[...], inverse[...], preferred_element_type=f32) * SCALE
        for row in range(12):
            for comp in range(3):
                at = 48 * (row // 4) + (32 + 4 * (row % 4) if comp == 2 else 8 * (row % 4) + 4 * comp)
                out[which, row // 3, row % 3, comp] = result[at : at + 4, :LAGS].astype(bf16)
        return carry

    lax.fori_loop(0, 2, side, 0)
    for cs in to_pair:
        wait_send(cs)

    @pl.when(above)
    def _():
        for cs in to_quad[0][2]:
            wait_send(cs)

    for _i, _peer, sent in to_quad[1:]:
        for cs in sent:
            wait_send(cs)
    wait_send(to_near)


def place_kernel(both, within, between, sems):
    copies = [pltpu.make_async_copy(both.at[k], out, sems.at[k]) for k, out in enumerate((within, between))]
    for c in copies:
        c.start()
    for c in copies:
        c.wait()


def shards(traces, assign, matching):
    anywhere = pl.BlockSpec(memory_space=pl.ANY)
    hbm = pl.BlockSpec(memory_space=pltpu.HBM)
    block = traces.shape
    assign = assign.reshape(1, 4)
    tables_ = [jnp.asarray(t) for t in tables()]
    result = (2, 4, 3, 3, 4, LAGS)
    both = pl.pallas_call(
        correlate_kernel,
        out_shape=jax.ShapeDtypeStruct(result, bf16),
        in_specs=[hbm] * 7,
        out_specs=pl.BlockSpec(memory_space=pltpu.VMEM),
        scratch_shapes=[
            pltpu.VMEM(block, bf16),
            pltpu.VMEM((2,) + block, bf16),
            pltpu.VMEM((4,) + block, bf16),
            pltpu.VMEM(block, bf16),
            pltpu.SMEM(matching.shape, jnp.int32),
            pltpu.SMEM((1, 4), jnp.int32),
            pltpu.SMEM((2, 1, 4), jnp.int32),
            pltpu.SMEM((4, 1, 4), jnp.int32),
            pltpu.SMEM((1, 4), jnp.int32),
            *(pltpu.VMEM(t.shape, t.dtype) for t in tables_),
            pltpu.VMEM((32, 1280), f32),
            *(pltpu.VMEM((32, NF), f32) for _ in range(4)),
            pltpu.VMEM((144, 2 * NF), bf16),
            pltpu.SemaphoreType.DMA((4 + 4 * STEP,)),
            pltpu.SemaphoreType.DMA((11,)),
            pltpu.SemaphoreType.REGULAR((5,)),
        ],
        compiler_params=pltpu.CompilerParams(collective_id=0, has_side_effects=True, vmem_limit_bytes=32 << 20),
        name="correlate",
    )(*(pltpu.with_memory_space_constraint(v, pltpu.HBM) for v in (traces, assign, matching, *tables_)))
    within, between = pl.pallas_call(
        place_kernel,
        out_shape=(jax.ShapeDtypeStruct(result[1:], bf16),) * 2,
        in_specs=[anywhere],
        out_specs=(anywhere, anywhere),
        scratch_shapes=[pltpu.SemaphoreType.DMA((2,))],
        compiler_params=pltpu.CompilerParams(vmem_limit_bytes=16 << 20),
        name="place",
    )(both)
    return tuple(jnp.transpose(v, (0, 3, 1, 2, 4)) for v in (between, within))


def solution(mesh):
    placed = (P(("group", "blk"), None, None, None), P(("group", "blk")), P("blk", None))
    return jax.shard_map(
        shards,
        mesh=mesh,
        in_specs=placed,
        out_specs=(
            P(("group", "blk"), None, None, None, None),
            P(("group", "blk"), None, None, None, None),
        ),
        check_vma=False,
    )
```
